128 devices in a mesh: front: 8 (over z, core), row: 4 (over y), col: 4 (over x).
Axes of the slice: x: 4, y: 4, z: 4, core: 2. Of those that a mesh axis runs over, the one named last changes fastest.
Arguments:
- child_fronts: float32 [128, 1536, 1536], P(('front', 'row', 'col')), may hold values from -6 to 103.97959, as said below
- parent_entries: float32 [8, 4096, 4096], P('front', 'row', 'col'), may hold values from -6 to 166, as said below
- tile_map: int32 [128, 8], P(('front', 'row', 'col')), may hold values from 0 to 31, as said below
- parent_group: int32 [128], P(('front', 'row', 'col')), may hold values from 0 to 7, as said below
Outputs:
- child_factor: float32 [128, 1536, 512], P(('front', 'row', 'col'))
- parent_factor: float32 [8, 4096, 4096], P('front', 'row', 'col')
The draws below stay inside these ranges and needn't reach their ends.
Inputs may be any that keep to these rules, and one draw needn't show every extreme that they name: `child_fronts`: each child front is symmetric positive definite. `parent_entries`: each parent's entries are symmetric, and every assembled parent front is positive definite. `tile_map`: each row is increasing and names exactly 2 tiles among each 8 consecutive tile numbers that start at a multiple of 8. `parent_group`: children are numbered in the order of the devices; in each run of 16 consecutive children, exactly 2 have each parent.
All inputs are finite; a program needn't handle non-finite values.
Results may differ from the reference program's by a relative error of at most 0.0001.
Values sent between devices are 32-bit elements; how exact they have to be, the bound alone decides.
No kernel may reach another device: no remote copies, remote signals or barrier semaphores. Data moves between devices by JAX's collectives and lax.ppermute only.
A program may use at most 192 MiB of HBM per device.

```python
import jax
import jax.numpy as jnp
from jax import lax

TILE = 128
K = 512
B = 1024
P_SIZE = 4096
E = 1024
G = 8
CHILDREN = 128
BT = 8
PTD = 8
MAPPER = 2
NPER = 2
N_ROW = 4


def symmetric_front(key, count, order):
    noise = jnp.clip(jax.random.normal(key, (count, order, order), jnp.float32), -4.0, 4.0)
    symmetric = (noise + jnp.swapaxes(noise, 1, 2)) * 0.70710678
    return symmetric + 2.5 * order ** 0.5 * jnp.eye(order, dtype=jnp.float32)[None]


def draw_child_fronts(key, part):
    return symmetric_front(jax.random.fold_in(key, 11), CHILDREN, K + B)


def draw_parent_entries(key, part):
    return symmetric_front(jax.random.fold_in(key, 23), G, P_SIZE)


def draw_tile_map(key, part):
    keys_list = jax.random.split(jax.random.fold_in(key, 37), CHILDREN * N_ROW)

    def choose(one_key):
        return jnp.sort(jax.random.permutation(one_key, PTD)[:MAPPER])
    picked = jax.vmap(choose)(keys_list).reshape(CHILDREN, N_ROW, MAPPER).astype(jnp.int32)
    starts = (jnp.arange(N_ROW, dtype=jnp.int32) * PTD)[None, :, None]
    return (picked + starts).reshape(CHILDREN, BT)


def draw_parent_group(key, part):
    slices = CHILDREN // (NPER * G)
    keys_list = jax.random.split(jax.random.fold_in(key, 53), slices)
    pattern = jnp.repeat(jnp.arange(G, dtype=jnp.int32), NPER)

    def shuffle(one_key):
        return jax.random.permutation(one_key, pattern)
    return jax.vmap(shuffle)(keys_list).reshape(CHILDREN).astype(jnp.int32)


def setup_inputs(seed: int = 0) -> dict:
    keys = jax.random.split(jax.random.key(seed), 5)
    return {
        "child_fronts": draw_child_fronts(jax.random.fold_in(keys[4], 71), 0),
        "parent_entries": draw_parent_entries(jax.random.fold_in(keys[4], 71), 0),
        "tile_map": draw_tile_map(jax.random.fold_in(keys[4], 71), 0),
        "parent_group": draw_parent_group(jax.random.fold_in(keys[4], 71), 0),
    }


def right_solve(pivot_factor, matrix):
    return lax.linalg.triangular_solve(pivot_factor, matrix, left_side=False, lower=True, transpose_a=True)

def factor_child(child_front):
    corner = child_front[:K, :K]
    border_cols = child_front[K:, :K]
    border_block = child_front[K:, K:]
    pivot_factor = jnp.linalg.cholesky(corner)
    child_panel = right_solve(pivot_factor, border_cols)
    update = border_block - jnp.dot(child_panel, child_panel.T, precision=lax.Precision.HIGHEST)
    return (jnp.concatenate([pivot_factor, child_panel], 0), update)

def eliminate(assembled):
    pivot_factor = jnp.linalg.cholesky(assembled[:E, :E])
    panel = right_solve(pivot_factor, assembled[E:, :E])
    trailing = assembled[E:, E:] - jnp.dot(panel, panel.T, precision=lax.Precision.HIGHEST)
    upper = jnp.concatenate([pivot_factor, panel.T], 1)
    bottom = jnp.concatenate([panel, trailing], 1)
    return jnp.concatenate([upper, bottom], 0)

def reference(child_fronts, parent_entries, tile_map, parent_group):
    offsets = jnp.arange(TILE, dtype=jnp.int32)

    def one_child(child, carry):
        parents, factors = carry
        factor, update = factor_child(child_fronts[child])
        factors = factors.at[child].set(factor)
        row_index = (tile_map[child][:, None] * TILE + offsets[None, :]).reshape(-1).astype(jnp.int32)
        parent_id = parent_group[child]
        parents = parents.at[parent_id, row_index[:, None], row_index[None, :]].add(update)
        return (parents, factors)
    factors = jnp.zeros((CHILDREN, K + B, K), jnp.float32)
    parents, factors = lax.fori_loop(0, CHILDREN, one_child, (parent_entries, factors))
    return (factors, lax.map(eliminate, parents))
```

```python
import jax
import jax.numpy as jnp
from jax import lax
from jax.experimental import pallas as pl
from jax.experimental.pallas import tpu as pltpu
from jax.sharding import PartitionSpec as P

TILE = 128
F32 = jnp.float32
BF16 = jnp.bfloat16
VMEM = pl.BlockSpec(memory_space=pltpu.VMEM)
SMEM = pl.BlockSpec(memory_space=pltpu.SMEM)
ANY = pl.BlockSpec(memory_space=pl.ANY)
K = 512
B = 1024
E = 1024
N_COL = 4
PIECE = B // N_COL
PANEL_OFF = TILE // N_COL
CORNER_OFF = TILE // (N_COL * N_COL)
SHARE_ROWS = 4 * PANEL_OFF + 2 * CORNER_OFF
LOWER = [(t, u) for t in range(8) for u in range(t + 1)]


def split(x):
    hi = x.astype(BF16)
    return hi, (x - hi.astype(F32)).astype(BF16)


def dot3(a, b, dims):
    def one(x, y):
        return lax.dot_general(x, y, (dims, ((), ())), preferred_element_type=F32)

    return one(a[0], b[0]) + (one(a[0], b[1]) + one(a[1], b[0]))


NT = ((1,), (1,))
NN = ((1,), (0,))


def factor_tile(tile_ref, u_ref, inv_ref):
    count = TILE // 8
    lane = lax.broadcasted_iota(jnp.int32, (8, TILE), 1)
    sub = lax.broadcasted_iota(jnp.int32, (8, TILE), 0)
    rows = [tile_ref[8 * g : 8 * g + 8, :] for g in range(count)]

    def full(x):
        return jnp.broadcast_to(x, (8, TILE))

    for group in range(count):
        top = rows[group]
        base = 8 * group
        below = range(group + 1, count)
        lead = [full(top[:, base + k : base + k + 1]) for k in range(8)]
        e = {(m, k): full(lead[k][m : m + 1, :]) for k in range(8) for m in range(k, 8)}
        pivots = (lane >= base) & (lane < base + 8)
        unit = jnp.where(pivots, jnp.where(lane == sub + base, 1.0, 0.0), top)
        r = [full(top[k : k + 1, :]) for k in range(8)]
        w = [full(unit[k : k + 1, :]) for k in range(8)]
        c = {(g, k): full(rows[g][:, base + k : base + k + 1]) for g in below for k in range(8)}
        new = {g: jnp.where(pivots, 0.0, rows[g]) for g in below}
        for k in range(8):
            scale = lax.rsqrt(e[k, k])
            l = {m: e[m, k] * scale for m in range(k + 1, 8)}
            for m in range(k + 1, 8):
                for q in range(k + 1, m + 1):
                    e[m, q] = e[m, q] - l[m] * l[q]
            r[k] = r[k] * scale
            w[k] = w[k] * scale
            for m in range(k + 1, 8):
                r[m] = r[m] - l[m] * r[k]
                w[m] = w[m] - l[m] * w[k]
            for g in below:
                column = c[g, k] * scale
                for m in range(k + 1, 8):
                    c[g, m] = c[g, m] - l[m] * column
                new[g] = new[g] - column * w[k]
        u, v = r[0], w[0]
        for k in range(1, 8):
            u = jnp.where(sub == k, r[k], u)
            v = jnp.where(sub == k, w[k], v)
        u_ref[base : base + 8, :] = jnp.where(lane >= sub + base, u, 0.0)
        inv_ref[base : base + 8, :] = jnp.where(lane <= sub + base, v, 0.0)
        for g in below:
            rows[g] = new[g]


def factor_columns(a_ref, l_ref, hi_ref, lo_ref, col_ref, tile_ref, u_ref, inv_ref, begin, done):
    rows, order = l_ref.shape
    blocks = order // TILE

    def step(kb, carry):
        for b in range(blocks):

            @pl.when(kb == b)
            def _(b=b):
                at = b * TILE
                begin(b)
                col = a_ref[at:, at : at + TILE]
                if b:
                    left = (hi_ref[at:, :at], lo_ref[at:, :at])
                    right = (hi_ref[at : at + TILE, :at], lo_ref[at : at + TILE, :at])
                    col = col - dot3(left, right, NT)
                tile_ref[...] = col[:TILE]
                if at + TILE < rows:
                    col_ref[at + TILE :, :] = col[TILE:]

        factor_tile(tile_ref, u_ref, inv_ref)
        for b in range(blocks):

            @pl.when(kb == b)
            def _(b=b):
                at = b * TILE
                if b:
                    l_ref[:at, at : at + TILE] = jnp.zeros((at, TILE), F32)
                l_ref[at : at + TILE, at : at + TILE] = u_ref[...].T
                if at + TILE < rows:
                    panel = dot3(split(col_ref[at + TILE :, :]), split(inv_ref[...]), NT)
                    l_ref[at + TILE :, at : at + TILE] = panel
                    hi, lo = split(panel)
                    hi_ref[at + TILE :, at : at + TILE] = hi
                    lo_ref[at + TILE :, at : at + TILE] = lo
                done(b)

        return carry

    lax.fori_loop(0, blocks, step, 0)


def child_kernel(front, factor, share, a, row_c, col_c, l, hi, lo, col, tile, u, inv, in_sem, out_sem):
    loads = [
        pltpu.make_async_copy(
            front.at[:, b * TILE : (b + 1) * TILE], a.at[:, b * TILE : (b + 1) * TILE], in_sem.at[b]
        )
        for b in range(4)
    ]
    loads.append(pltpu.make_async_copy(front.at[K : K + PIECE, K : K + B], row_c, in_sem.at[4]))
    loads.append(pltpu.make_async_copy(front.at[K : K + B, K : K + PIECE], col_c, in_sem.at[5]))
    for load in loads:
        load.start()
    stores = [
        pltpu.make_async_copy(
            l.at[:, b * TILE : (b + 1) * TILE], factor.at[:, b * TILE : (b + 1) * TILE], out_sem.at[b]
        )
        for b in range(4)
    ]
    factor_columns(
        a, l, hi, lo, col, tile, u, inv, lambda b: loads[b].wait(), lambda b: stores[b].start()
    )
    loads[4].wait()
    loads[5].wait()
    head = (hi[K : K + PIECE, :], lo[K : K + PIECE, :])
    every = (hi[K:, :], lo[K:, :])
    row_c[...] = row_c[...] - dot3(head, every, NT)
    col_c[...] = col_c[...] - dot3(every, head, NT)
    for i in range(4):
        for j in range(4):
            s = 4 * i + j
            for h in range(2):
                at = i * PIECE + h * TILE + j * PANEL_OFF
                share[s, h * PANEL_OFF : (h + 1) * PANEL_OFF, :] = col_c[at : at + PANEL_OFF, :]
                at = h * TILE + i * PANEL_OFF
                share[s, (2 + h) * PANEL_OFF : (3 + h) * PANEL_OFF, :] = row_c[
                    at : at + PANEL_OFF, j * PIECE : (j + 1) * PIECE
                ]
                at = h * TILE + (4 * j + i) * CORNER_OFF
                to = 4 * PANEL_OFF + h * CORNER_OFF
                share[s, to : to + CORNER_OFF, :] = col_c[at : at + CORNER_OFF, :]
    for store in stores:
        store.wait()


def child_call(front):
    order = front.shape[0]
    return pl.pallas_call(
        child_kernel,
        name="child_factor",
        in_specs=[ANY],
        out_specs=[ANY, VMEM],
        out_shape=[
            jax.ShapeDtypeStruct((order, K), F32),
            jax.ShapeDtypeStruct((16, SHARE_ROWS, PIECE), F32),
        ],
        scratch_shapes=[
            pltpu.VMEM((order, K), F32),
            pltpu.VMEM((PIECE, B), F32),
            pltpu.VMEM((B, PIECE), F32),
            pltpu.VMEM((order, K), F32),
            pltpu.VMEM((order, K), BF16),
            pltpu.VMEM((order, K), BF16),
            pltpu.VMEM((order, TILE), F32),
            pltpu.VMEM((TILE, TILE), F32),
            pltpu.VMEM((TILE, TILE), F32),
            pltpu.VMEM((TILE, TILE), F32),
            pltpu.SemaphoreType.DMA((6,)),
            pltpu.SemaphoreType.DMA((4,)),
        ],
    )(front)


def update_kernel(panel, border, pieces):
    part = split(panel[...])
    z = border[...] - dot3(part, part, NT)
    for i in range(3):
        for j in range(3):
            pieces[4 * (i + 1) + j + 1] = z[
                i * PIECE : (i + 1) * PIECE, j * PIECE : (j + 1) * PIECE
            ]


def update_call(front, factor):
    inner = B - PIECE
    at = front.shape[0] // inner - 1
    return pl.pallas_call(
        update_kernel,
        name="child_update",
        grid=(1,),
        in_specs=[
            pl.BlockSpec((inner, K), lambda i: (at, 0)),
            pl.BlockSpec((inner, inner), lambda i: (at, at)),
        ],
        out_specs=pl.BlockSpec((16, PIECE, PIECE), lambda i: (0, 0, 0)),
        out_shape=jax.ShapeDtypeStruct((16, PIECE, PIECE), F32),
    )(factor, front)


def route_kernel(here, table, slots, kids, counts):
    front = here[0]
    for g in range(8):
        counts[g] = 0

    def place(c, carry):
        g = table[front * 16 + c, 8]
        slots[c] = 2 * g + counts[g]
        counts[g] = counts[g] + 1
        return carry

    lax.fori_loop(0, 16, place, 0)

    def pick(c, n):
        mine = table[c, 8] == front

        @pl.when(mine)
        def _():
            for b in range(8):
                kids[n, b] = table[c, b]

        return n + jnp.where(mine, 1, 0)

    lax.fori_loop(0, 128, pick, 0)


def route_call(here, table):
    return pl.pallas_call(
        route_kernel,
        name="route",
        in_specs=[SMEM, SMEM],
        out_specs=[SMEM, SMEM],
        out_shape=[
            jax.ShapeDtypeStruct((16,), jnp.int32),
            jax.ShapeDtypeStruct((16, 8), jnp.int32),
        ],
        scratch_shapes=[pltpu.SMEM((8,), jnp.int32)],
    )(here, table)


def regroup_kernel(slots, source, target, sem):
    copies = [
        pltpu.make_async_copy(source.at[c], target.at[slots[c]], sem.at[c]) for c in range(16)
    ]
    for copy in copies:
        copy.start()
    for copy in copies:
        copy.wait()


def regroup_call(slots, source):
    return pl.pallas_call(
        regroup_kernel,
        name="regroup",
        in_specs=[SMEM, ANY],
        out_specs=ANY,
        out_shape=jax.ShapeDtypeStruct(source.shape, source.dtype),
        scratch_shapes=[pltpu.SemaphoreType.DMA((16,))],
    )(slots, source)


def share_kernel(here, kids, landed, row_e, col_e, corner_e, row_out, col_out, corner_out):
    row = here[1]
    col = here[2]
    row_out[...] = row_e[0]
    col_out[...] = col_e[0]
    for n, (t, u) in enumerate(LOWER):
        corner_out[n] = corner_e[0, t, :, u * TILE : (u + 1) * TILE]

    def add(n, carry):
        for h in range(2):
            for v in range(2):
                lanes = slice(v * TILE, (v + 1) * TILE)
                t = kids[n, 2 * row + h] - 8 * row
                u = pl.ds(pl.multiple_of(kids[n, v] * TILE, TILE), TILE)
                row_out[t, :, u] += landed[n, h * PANEL_OFF : (h + 1) * PANEL_OFF, lanes]
                t = kids[n, h]
                u = pl.ds(pl.multiple_of((kids[n, 2 * col + v] - 8 * col) * TILE, TILE), TILE)
                col_out[t, :, u] += landed[n, (2 + h) * PANEL_OFF : (3 + h) * PANEL_OFF, lanes]
                if v <= h:
                    at = 4 * PANEL_OFF + h * CORNER_OFF
                    index = lax.shift_right_logical(t * (t + 1), 1) + kids[n, v]
                    corner_out[index] += landed[n, at : at + CORNER_OFF, lanes]
        return carry

    lax.fori_loop(0, 16, add, 0)


def share_call(here, kids, landed, row_e, col_e, corner_e):
    def first(shape):
        return pl.BlockSpec((1, *shape[1:]), lambda i: (0,) * len(shape))

    def whole(shape):
        return pl.BlockSpec(shape, lambda i: (0,) * len(shape))

    panel = row_e.shape[1:]
    corner = (len(LOWER), CORNER_OFF, TILE)
    return pl.pallas_call(
        share_kernel,
        name="share_assembly",
        grid=(1,),
        in_specs=[
            SMEM,
            SMEM,
            whole(landed.shape),
            first(row_e.shape),
            first(col_e.shape),
            first(corner_e.shape),
        ],
        out_specs=[whole(panel), whole(panel), whole(corner)],
        out_shape=[
            jax.ShapeDtypeStruct(panel, F32),
            jax.ShapeDtypeStruct(panel, F32),
            jax.ShapeDtypeStruct(corner, F32),
        ],
    )(here, kids, landed, row_e, col_e, corner_e)


def corner_kernel(parts, l, invs, a, hi, lo, col, tile, u, inv):
    for d in range(16):
        off = (4 * (d % 4) + d // 4) * CORNER_OFF
        for n, (t, v) in enumerate(LOWER):
            at = t * TILE + off
            a[at : at + CORNER_OFF, v * TILE : (v + 1) * TILE] = parts[d, n]

    def done(b):
        invs[b] = inv[...]

    factor_columns(a, l, hi, lo, col, tile, u, inv, lambda b: None, done)


def corner_call(parts):
    return pl.pallas_call(
        corner_kernel,
        name="corner_factor",
        in_specs=[VMEM],
        out_specs=[VMEM, VMEM],
        out_shape=[
            jax.ShapeDtypeStruct((E, E), F32),
            jax.ShapeDtypeStruct((E // TILE, TILE, TILE), F32),
        ],
        scratch_shapes=[
            pltpu.VMEM((E, E), F32),
            pltpu.VMEM((E, E), BF16),
            pltpu.VMEM((E, E), BF16),
            pltpu.VMEM((E, TILE), F32),
            pltpu.VMEM((TILE, TILE), F32),
            pltpu.VMEM((TILE, TILE), F32),
            pltpu.VMEM((TILE, TILE), F32),
        ],
    )(parts)


def solve_kernel(l, invs, row_parts, col_parts, w, y, a, b, whi, wlo, yhi, ylo):
    for q in range(4):
        for t in range(8):
            at = t * TILE + q * PANEL_OFF
            a[at : at + PANEL_OFF, :] = row_parts[q, t]
            b[at : at + PANEL_OFF, :] = col_parts[q, t]
    for k in range(E // TILE):
        at = k * TILE
        here = slice(at, at + TILE)
        inv = split(invs[k])
        left = a[:, here]
        right = b[here, :]
        if k:
            lower = split(l[here, :at])
            left = left - dot3((whi[:, :at], wlo[:, :at]), lower, NT)
            right = right - dot3(lower, (yhi[:at, :], ylo[:at, :]), NN)
        left = dot3(split(left), inv, NT)
        right = dot3(inv, split(right), NN)
        w[:, here] = left
        y[here, :] = right
        whi[:, here], wlo[:, here] = split(left)
        yhi[here, :], ylo[here, :] = split(right)


def solve_call(l, invs, row_parts, col_parts):
    return pl.pallas_call(
        solve_kernel,
        name="panel_solve",
        in_specs=[VMEM] * 4,
        out_specs=[VMEM, VMEM],
        out_shape=[jax.ShapeDtypeStruct((B, E), F32), jax.ShapeDtypeStruct((E, B), F32)],
        scratch_shapes=[pltpu.VMEM((B, E), F32)] * 2 + [pltpu.VMEM((B, E), BF16)] * 4,
    )(l, invs, row_parts, col_parts)


def final_kernel(here, kids, entries, landed, l, w, y, out):
    row = here[1]
    col = here[2]

    @pl.when((row == 0) & (col == 0))
    def _():
        out[...] = l[...]

    @pl.when((row != 0) & (col == 0))
    def _():
        out[...] = w[...]

    @pl.when((row == 0) & (col != 0))
    def _():
        out[...] = y[...]

    @pl.when((row != 0) & (col != 0))
    def _():
        out[...] = entries[...] - dot3(split(w[...]), split(y[...]), NN)

        def add(n, carry):
            for h in range(2):
                for v in range(2):
                    t = (kids[n, 2 * row + h] - 8 * row) * TILE
                    u = (kids[n, 2 * col + v] - 8 * col) * TILE
                    out[pl.ds(pl.multiple_of(t, TILE), TILE), pl.ds(pl.multiple_of(u, TILE), TILE)] += (
                        landed[n, h * TILE : (h + 1) * TILE, v * TILE : (v + 1) * TILE]
                    )
            return carry

        lax.fori_loop(0, 16, add, 0)


def final_call(here, kids, entries, landed, l, w, y):
    return pl.pallas_call(
        final_kernel,
        name="trailing",
        in_specs=[SMEM, SMEM] + [VMEM] * 5,
        out_specs=VMEM,
        out_shape=jax.ShapeDtypeStruct(entries.shape, F32),
    )(here, kids, entries, landed, l, w, y)


def exchange(array, axes):
    return lax.all_to_all(array, axes, split_axis=0, concat_axis=0, tiled=True)


def local(child_fronts, parent_entries, tile_map, parent_group):
    plane = ("row", "col")
    front = child_fronts[0]
    entries = parent_entries[0]
    here = jnp.stack([lax.axis_index(name) for name in ("front", "row", "col")]).astype(jnp.int32)
    label = jnp.concatenate([tile_map[0], parent_group, jnp.zeros((7,), jnp.int32)])
    table = lax.all_gather(label.astype(F32), ("front", "row", "col")).astype(jnp.int32)
    slots, kids = route_call(here, table)
    by_offset = entries.reshape(8, 4, PANEL_OFF, B).transpose(1, 0, 2, 3)
    row_e = exchange(by_offset, "col")
    col_e = exchange(by_offset, "row")
    corner_e = exchange(
        row_e[0].reshape(8, 4, CORNER_OFF, B).transpose(1, 0, 2, 3), "row"
    )
    factor, share = child_call(front)
    pieces = update_call(front, factor)
    share_near = exchange(share, plane)
    share_far = exchange(regroup_call(slots, share_near), "front")
    pieces_near = exchange(pieces, plane)
    pieces_far = exchange(regroup_call(slots, pieces_near), "front")
    row_own, col_own, corner_own = share_call(here, kids, share_far, row_e, col_e, corner_e)
    corner_parts = lax.all_gather(corner_own, plane)
    row_parts = lax.all_gather(row_own, "col")
    col_parts = lax.all_gather(col_own, "row")
    l, invs = corner_call(corner_parts)
    w, y = solve_call(l, invs, row_parts, col_parts)
    result = final_call(here, kids, entries, pieces_far, l, w, y)
    return (factor[None], result[None])


def solution(mesh):
    in_specs = (
        P(("front", "row", "col"), None, None),
        P("front", "row", "col"),
        P(("front", "row", "col"), None),
        P(("front", "row", "col")),
    )
    out_specs = (P(("front", "row", "col"), None, None), P("front", "row", "col"))
    return jax.shard_map(local, mesh=mesh, in_specs=in_specs, out_specs=out_specs, check_vma=False)
```

```python
import jax
import jax.numpy as jnp
from jax import lax
from jax.experimental import pallas as pl
from jax.experimental.pallas import tpu as pltpu
from jax.sharding import PartitionSpec as P


TILE = 128
F32 = jnp.float32
BF16 = jnp.bfloat16
VMEM = pl.BlockSpec(memory_space=pltpu.VMEM)
SMEM = pl.BlockSpec(memory_space=pltpu.SMEM)
ANY = pl.BlockSpec(memory_space=pl.ANY)
K = 512
B = 1024
E = 1024
N_COL = 4
PIECE = B // N_COL
PANEL_OFF = TILE // N_COL
CORNER_OFF = TILE // (N_COL * N_COL)
LABEL_ROW = 4 * PANEL_OFF + 2 * CORNER_OFF
SHARE_ROWS = LABEL_ROW + 8
LOWER = [(t, u) for t in range(8) for u in range(t + 1)]


def split(x):
    hi = x.astype(BF16)
    return hi, (x - hi.astype(F32)).astype(BF16)


def dot3(a, b, dims):
    def one(x, y):
        return lax.dot_general(x, y, (dims, ((), ())), preferred_element_type=F32)

    return one(a[0], b[0]) + (one(a[0], b[1]) + one(a[1], b[0]))


NT = ((1,), (1,))
NN = ((1,), (0,))


def factor_tile(tile_ref, u_ref, inv_ref):
    count = TILE // 8
    lane = lax.broadcasted_iota(jnp.int32, (8, TILE), 1)
    sub = lax.broadcasted_iota(jnp.int32, (8, TILE), 0)
    rows = [tile_ref[8 * g : 8 * g + 8, :] for g in range(count)]

    def full(x):
        return jnp.broadcast_to(x, (8, TILE))

    for group in range(count):
        top = rows[group]
        base = 8 * group
        below = range(group + 1, count)
        lead = [full(top[:, base + k : base + k + 1]) for k in range(8)]
        e = {(m, k): full(lead[k][m : m + 1, :]) for k in range(8) for m in range(k, 8)}
        pivots = (lane >= base) & (lane < base + 8)
        unit = jnp.where(pivots, jnp.where(lane == sub + base, 1.0, 0.0), top)
        r = [full(top[k : k + 1, :]) for k in range(8)]
        w = [full(unit[k : k + 1, :]) for k in range(8)]
        c = {(g, k): full(rows[g][:, base + k : base + k + 1]) for g in below for k in range(8)}
        new = {g: jnp.where(pivots, 0.0, rows[g]) for g in below}
        for k in range(8):
            scale = lax.rsqrt(e[k, k])
            l = {m: e[m, k] * scale for m in range(k + 1, 8)}
            for m in range(k + 1, 8):
                for q in range(k + 1, m + 1):
                    e[m, q] = e[m, q] - l[m] * l[q]
            r[k] = r[k] * scale
            w[k] = w[k] * scale
            for m in range(k + 1, 8):
                r[m] = r[m] - l[m] * r[k]
                w[m] = w[m] - l[m] * w[k]
            for g in below:
                column = c[g, k] * scale
                for m in range(k + 1, 8):
                    c[g, m] = c[g, m] - l[m] * column
                new[g] = new[g] - column * w[k]
        u, v = r[0], w[0]
        for k in range(1, 8):
            u = jnp.where(sub == k, r[k], u)
            v = jnp.where(sub == k, w[k], v)
        u_ref[base : base + 8, :] = jnp.where(lane >= sub + base, u, 0.0)
        inv_ref[base : base + 8, :] = jnp.where(lane <= sub + base, v, 0.0)
        for g in below:
            rows[g] = new[g]


def factor_columns(a_ref, l_ref, hi_ref, lo_ref, col_ref, tile_ref, u_ref, inv_ref, begin, done):
    rows, order = l_ref.shape
    blocks = order // TILE

    def step(kb, carry):
        for b in range(blocks):

            @pl.when(kb == b)
            def _(b=b):
                at = b * TILE
                begin(b)
                col = a_ref[at:, at : at + TILE]
                if b:
                    left = (hi_ref[at:, :at], lo_ref[at:, :at])
                    right = (hi_ref[at : at + TILE, :at], lo_ref[at : at + TILE, :at])
                    col = col - dot3(left, right, NT)
                tile_ref[...] = col[:TILE]
                if at + TILE < rows:
                    col_ref[at + TILE :, :] = col[TILE:]

        factor_tile(tile_ref, u_ref, inv_ref)
        for b in range(blocks):

            @pl.when(kb == b)
            def _(b=b):
                at = b * TILE
                if b:
                    l_ref[:at, at : at + TILE] = jnp.zeros((at, TILE), F32)
                l_ref[at : at + TILE, at : at + TILE] = u_ref[...].T
                if at + TILE < rows:
                    panel = dot3(split(col_ref[at + TILE :, :]), split(inv_ref[...]), NT)
                    l_ref[at + TILE :, at : at + TILE] = panel
                    hi, lo = split(panel)
                    hi_ref[at + TILE :, at : at + TILE] = hi
                    lo_ref[at + TILE :, at : at + TILE] = lo
                done(b)

        return carry

    lax.fori_loop(0, blocks, step, 0)


def child_kernel(front, label, factor, share, a, row_c, col_c, l, hi, lo, col, tile, u, inv, in_sem, out_sem):
    loads = [
        pltpu.make_async_copy(
            front.at[:, b * TILE : (b + 1) * TILE], a.at[:, b * TILE : (b + 1) * TILE], in_sem.at[b]
        )
        for b in range(4)
    ]
    loads.append(pltpu.make_async_copy(front.at[K : K + PIECE, K : K + B], row_c, in_sem.at[4]))
    loads.append(pltpu.make_async_copy(front.at[K : K + B, K : K + PIECE], col_c, in_sem.at[5]))
    for load in loads:
        load.start()
    stores = [
        pltpu.make_async_copy(
            l.at[:, b * TILE : (b + 1) * TILE], factor.at[:, b * TILE : (b + 1) * TILE], out_sem.at[b]
        )
        for b in range(4)
    ]
    factor_columns(
        a, l, hi, lo, col, tile, u, inv, lambda b: loads[b].wait(), lambda b: stores[b].start()
    )
    loads[4].wait()
    loads[5].wait()
    head = (hi[K : K + PIECE, :], lo[K : K + PIECE, :])
    every = (hi[K:, :], lo[K:, :])
    row_c[...] = row_c[...] - dot3(head, every, NT)
    col_c[...] = col_c[...] - dot3(every, head, NT)
    for i in range(4):
        for j in range(4):
            s = 4 * i + j
            for h in range(2):
                at = i * PIECE + h * TILE + j * PANEL_OFF
                share[s, h * PANEL_OFF : (h + 1) * PANEL_OFF, :] = col_c[at : at + PANEL_OFF, :]
                at = h * TILE + i * PANEL_OFF
                share[s, (2 + h) * PANEL_OFF : (3 + h) * PANEL_OFF, :] = row_c[
                    at : at + PANEL_OFF, j * PIECE : (j + 1) * PIECE
                ]
                at = h * TILE + (4 * j + i) * CORNER_OFF
                to = 4 * PANEL_OFF + h * CORNER_OFF
                share[s, to : to + CORNER_OFF, :] = col_c[at : at + CORNER_OFF, :]
            share[s, LABEL_ROW:, :] = label[...]
    for store in stores:
        store.wait()


def child_call(front, label):
    order = front.shape[0]
    return pl.pallas_call(
        child_kernel,
        name="child_factor",
        in_specs=[ANY, VMEM],
        out_specs=[ANY, VMEM],
        out_shape=[
            jax.ShapeDtypeStruct((order, K), F32),
            jax.ShapeDtypeStruct((16, SHARE_ROWS, PIECE), F32),
        ],
        scratch_shapes=[
            pltpu.VMEM((order, K), F32),
            pltpu.VMEM((PIECE, B), F32),
            pltpu.VMEM((B, PIECE), F32),
            pltpu.VMEM((order, K), F32),
            pltpu.VMEM((order, K), BF16),
            pltpu.VMEM((order, K), BF16),
            pltpu.VMEM((order, TILE), F32),
            pltpu.VMEM((TILE, TILE), F32),
            pltpu.VMEM((TILE, TILE), F32),
            pltpu.VMEM((TILE, TILE), F32),
            pltpu.SemaphoreType.DMA((6,)),
            pltpu.SemaphoreType.DMA((4,)),
        ],
    )(front, label)


def update_kernel(panel, border, pieces):
    part = split(panel[...])
    z = border[...] - dot3(part, part, NT)
    for i in range(3):
        for j in range(3):
            pieces[4 * (i + 1) + j + 1] = z[
                i * PIECE : (i + 1) * PIECE, j * PIECE : (j + 1) * PIECE
            ]


def update_call(front, factor):
    inner = B - PIECE
    at = front.shape[0] // inner - 1
    return pl.pallas_call(
        update_kernel,
        name="child_update",
        grid=(1,),
        in_specs=[
            pl.BlockSpec((inner, K), lambda i: (at, 0)),
            pl.BlockSpec((inner, inner), lambda i: (at, at)),
        ],
        out_specs=pl.BlockSpec((16, PIECE, PIECE), lambda i: (0, 0, 0)),
        out_shape=jax.ShapeDtypeStruct((16, PIECE, PIECE), F32),
    )(factor, front)


def regroup_kernel(labels, source, target, buffer, counts, in_sem, out_sem):
    for g in range(8):
        counts[g] = 0
    loads, stores = [], []
    for c in range(16):
        loads.append(pltpu.make_async_copy(source.at[c], buffer.at[c], in_sem.at[c]))
        loads[c].start()
    for c in range(16):
        g = labels[c, 8]
        slot = 2 * g + counts[g]
        counts[g] = counts[g] + 1
        loads[c].wait()
        stores.append(pltpu.make_async_copy(buffer.at[c], target.at[slot], out_sem.at[c]))
        stores[c].start()
    for c in range(16):
        stores[c].wait()


def regroup_call(labels, source):
    return pl.pallas_call(
        regroup_kernel,
        name="regroup",
        in_specs=[SMEM, ANY],
        out_specs=ANY,
        out_shape=jax.ShapeDtypeStruct(source.shape, source.dtype),
        scratch_shapes=[
            pltpu.VMEM(source.shape, source.dtype),
            pltpu.SMEM((8,), jnp.int32),
            pltpu.SemaphoreType.DMA((16,)),
            pltpu.SemaphoreType.DMA((16,)),
        ],
    )(labels, source)


def share_kernel(here, kids, landed, row_e, col_e, corner_e, row_out, col_out, corner_out):
    row = here[1]
    col = here[2]
    row_out[...] = row_e[0]
    col_out[...] = col_e[0]
    for n, (t, u) in enumerate(LOWER):
        corner_out[n] = corner_e[0, t, :, u * TILE : (u + 1) * TILE]

    def add(n, carry):
        for h in range(2):
            for v in range(2):
                lanes = slice(v * TILE, (v + 1) * TILE)
                t = kids[n, 2 * row + h] - 8 * row
                u = pl.ds(pl.multiple_of(kids[n, v] * TILE, TILE), TILE)
                row_out[t, :, u] += landed[n, h * PANEL_OFF : (h + 1) * PANEL_OFF, lanes]
                t = kids[n, h]
                u = pl.ds(pl.multiple_of((kids[n, 2 * col + v] - 8 * col) * TILE, TILE), TILE)
                col_out[t, :, u] += landed[n, (2 + h) * PANEL_OFF : (3 + h) * PANEL_OFF, lanes]
                if v <= h:
                    at = 4 * PANEL_OFF + h * CORNER_OFF
                    index = lax.shift_right_logical(t * (t + 1), 1) + kids[n, v]
                    corner_out[index] += landed[n, at : at + CORNER_OFF, lanes]
        return carry

    lax.fori_loop(0, 16, add, 0)


def share_call(here, kids, landed, row_e, col_e, corner_e):
    def first(shape):
        return pl.BlockSpec((1, *shape[1:]), lambda i: (0,) * len(shape))

    def whole(shape):
        return pl.BlockSpec(shape, lambda i: (0,) * len(shape))

    panel = row_e.shape[1:]
    corner = (len(LOWER), CORNER_OFF, TILE)
    return pl.pallas_call(
        share_kernel,
        name="share_assembly",
        grid=(1,),
        in_specs=[
            SMEM,
            SMEM,
            whole(landed.shape),
            first(row_e.shape),
            first(col_e.shape),
            first(corner_e.shape),
        ],
        out_specs=[whole(panel), whole(panel), whole(corner)],
        out_shape=[
            jax.ShapeDtypeStruct(panel, F32),
            jax.ShapeDtypeStruct(panel, F32),
            jax.ShapeDtypeStruct(corner, F32),
        ],
    )(here, kids, landed, row_e, col_e, corner_e)


def corner_kernel(parts, l, invs, a, hi, lo, col, tile, u, inv):
    for d in range(16):
        off = (4 * (d % 4) + d // 4) * CORNER_OFF
        for n, (t, v) in enumerate(LOWER):
            at = t * TILE + off
            a[at : at + CORNER_OFF, v * TILE : (v + 1) * TILE] = parts[d, n]

    def done(b):
        invs[b] = inv[...]

    factor_columns(a, l, hi, lo, col, tile, u, inv, lambda b: None, done)


def corner_call(parts):
    return pl.pallas_call(
        corner_kernel,
        name="corner_factor",
        in_specs=[VMEM],
        out_specs=[VMEM, VMEM],
        out_shape=[
            jax.ShapeDtypeStruct((E, E), F32),
            jax.ShapeDtypeStruct((E // TILE, TILE, TILE), F32),
        ],
        scratch_shapes=[
            pltpu.VMEM((E, E), F32),
            pltpu.VMEM((E, E), BF16),
            pltpu.VMEM((E, E), BF16),
            pltpu.VMEM((E, TILE), F32),
            pltpu.VMEM((TILE, TILE), F32),
            pltpu.VMEM((TILE, TILE), F32),
            pltpu.VMEM((TILE, TILE), F32),
        ],
    )(parts)


def solve_kernel(here, l, invs, *refs):
    row_parts, col_parts = refs[:4], refs[4:8]
    w, y, a, b, whi, wlo, yhi, ylo = refs[8:]
    for s in range(4):
        for target, parts, place in ((a, row_parts, here[2]), (b, col_parts, here[1])):
            off = ((place + 4 - s) & 3) * PANEL_OFF
            for t in range(8):
                at = pl.multiple_of(t * TILE + off, PANEL_OFF)
                target[pl.ds(at, PANEL_OFF), :] = parts[s][t]
    for k in range(E // TILE):
        at = k * TILE
        here = slice(at, at + TILE)
        inv = split(invs[k])
        left = a[:, here]
        right = b[here, :]
        if k:
            lower = split(l[here, :at])
            left = left - dot3((whi[:, :at], wlo[:, :at]), lower, NT)
            right = right - dot3(lower, (yhi[:at, :], ylo[:at, :]), NN)
        left = dot3(split(left), inv, NT)
        right = dot3(inv, split(right), NN)
        w[:, here] = left
        y[here, :] = right
        whi[:, here], wlo[:, here] = split(left)
        yhi[here, :], ylo[here, :] = split(right)


def solve_call(here, l, invs, row_parts, col_parts):
    return pl.pallas_call(
        solve_kernel,
        name="panel_solve",
        in_specs=[SMEM] + [VMEM] * 10,
        out_specs=[VMEM, VMEM],
        out_shape=[jax.ShapeDtypeStruct((B, E), F32), jax.ShapeDtypeStruct((E, B), F32)],
        scratch_shapes=[pltpu.VMEM((B, E), F32)] * 2 + [pltpu.VMEM((B, E), BF16)] * 4,
    )(here, l, invs, *row_parts, *col_parts)


def final_kernel(here, kids, entries, landed, l, w, y, out):
    row = here[1]
    col = here[2]

    @pl.when((row == 0) & (col == 0))
    def _():
        out[...] = l[...]

    @pl.when((row != 0) & (col == 0))
    def _():
        out[...] = w[...]

    @pl.when((row == 0) & (col != 0))
    def _():
        out[...] = y[...]

    @pl.when((row != 0) & (col != 0))
    def _():
        out[...] = entries[...] - dot3(split(w[...]), split(y[...]), NN)

        def add(n, carry):
            for h in range(2):
                for v in range(2):
                    t = (kids[n, 2 * row + h] - 8 * row) * TILE
                    u = (kids[n, 2 * col + v] - 8 * col) * TILE
                    out[pl.ds(pl.multiple_of(t, TILE), TILE), pl.ds(pl.multiple_of(u, TILE), TILE)] += (
                        landed[n, h * TILE : (h + 1) * TILE, v * TILE : (v + 1) * TILE]
                    )
            return carry

        lax.fori_loop(0, 16, add, 0)


def final_call(here, kids, entries, landed, l, w, y):
    return pl.pallas_call(
        final_kernel,
        name="trailing",
        in_specs=[SMEM, SMEM] + [VMEM] * 5,
        out_specs=VMEM,
        out_shape=jax.ShapeDtypeStruct(entries.shape, F32),
    )(here, kids, entries, landed, l, w, y)


def exchange(array, axes):
    return lax.all_to_all(array, axes, split_axis=0, concat_axis=0, tiled=True)


def shifts(array, axis):
    parts = [array]
    for s in range(1, 4):
        parts.append(lax.ppermute(array, axis, [(p, (p + s) % 4) for p in range(4)]))
    return parts


def program(child_fronts, parent_entries, tile_map, parent_group):
    plane = ("row", "col")
    front = child_fronts[0]
    entries = parent_entries[0]
    here = jnp.stack([lax.axis_index(name) for name in ("front", "row", "col")]).astype(jnp.int32)
    label = jnp.concatenate([tile_map[0], parent_group, jnp.zeros((PIECE - 9,), jnp.int32)])
    label = jnp.broadcast_to(label.astype(F32)[None], (8, PIECE))
    by_offset = entries.reshape(8, 4, PANEL_OFF, B).transpose(1, 0, 2, 3)
    row_e = exchange(by_offset, "col")
    col_e = exchange(by_offset, "row")
    corner_e = exchange(
        row_e[0].reshape(8, 4, CORNER_OFF, B).transpose(1, 0, 2, 3), "row"
    )
    factor, share = child_call(front, label)
    pieces = update_call(front, factor)
    share_near = exchange(share, plane)
    labels = share_near[:, LABEL_ROW, :16].astype(jnp.int32)
    share_near = regroup_call(labels, share_near)
    share_far = exchange(share_near, "front")
    kids = share_far[:, LABEL_ROW, :8].astype(jnp.int32)
    pieces_near = exchange(pieces, plane)
    pieces_near = regroup_call(labels, pieces_near)
    pieces_far = exchange(pieces_near, "front")
    row_own, col_own, corner_own = share_call(here, kids, share_far, row_e, col_e, corner_e)
    corner_parts = lax.all_gather(corner_own, plane)
    row_parts = shifts(row_own, "col")
    col_parts = shifts(col_own, "row")
    l, invs = corner_call(corner_parts)
    w, y = solve_call(here, l, invs, row_parts, col_parts)
    result = final_call(here, kids, entries, pieces_far, l, w, y)
    return (factor[None], result[None])


def solution(mesh):
    in_specs = (
        P(("front", "row", "col"), None, None),
        P("front", "row", "col"),
        P(("front", "row", "col"), None),
        P(("front", "row", "col")),
    )
    out_specs = (P(("front", "row", "col"), None, None), P("front", "row", "col"))
    return jax.shard_map(program, mesh=mesh, in_specs=in_specs, out_specs=out_specs, check_vma=False)
```

```python
import jax
import jax.numpy as jnp
from jax import lax
from jax.experimental import pallas as pl
from jax.experimental.pallas import tpu as pltpu
from jax.sharding import PartitionSpec as P


TILE = 128
F32 = jnp.float32
BF16 = jnp.bfloat16
VMEM = pl.BlockSpec(memory_space=pltpu.VMEM)
SMEM = pl.BlockSpec(memory_space=pltpu.SMEM)
ANY = pl.BlockSpec(memory_space=pl.ANY)
K = 512
B = 1024
E = 1024
N_COL = 4
PIECE = B // N_COL
PANEL_OFF = TILE // N_COL
CORNER_OFF = TILE // (N_COL * N_COL)
LABEL_ROW = 4 * PANEL_OFF + 2 * CORNER_OFF
SHARE_ROWS = LABEL_ROW + 8
LOWER = [(t, u) for t in range(8) for u in range(t + 1)]


def split(x):
    hi = x.astype(BF16)
    return hi, (x - hi.astype(F32)).astype(BF16)


def dot3(a, b, dims):
    def one(x, y):
        return lax.dot_general(x, y, (dims, ((), ())), preferred_element_type=F32)

    return one(a[0], b[0]) + (one(a[0], b[1]) + one(a[1], b[0]))


NT = ((1,), (1,))
NN = ((1,), (0,))


def factor_tile(tile_ref, u_ref, inv_ref):
    count = TILE // 8
    lane = lax.broadcasted_iota(jnp.int32, (8, TILE), 1)
    sub = lax.broadcasted_iota(jnp.int32, (8, TILE), 0)
    rows = [tile_ref[8 * g : 8 * g + 8, :] for g in range(count)]

    def full(x):
        return jnp.broadcast_to(x, (8, TILE))

    for group in range(count):
        top = rows[group]
        base = 8 * group
        below = range(group + 1, count)
        lead = [full(top[:, base + k : base + k + 1]) for k in range(8)]
        e = {(m, k): full(lead[k][m : m + 1, :]) for k in range(8) for m in range(k, 8)}
        pivots = (lane >= base) & (lane < base + 8)
        unit = jnp.where(pivots, jnp.where(lane == sub + base, 1.0, 0.0), top)
        r = [full(top[k : k + 1, :]) for k in range(8)]
        w = [full(unit[k : k + 1, :]) for k in range(8)]
        c = {(g, k): full(rows[g][:, base + k : base + k + 1]) for g in below for k in range(8)}
        new = {g: jnp.where(pivots, 0.0, rows[g]) for g in below}
        for k in range(8):
            scale = lax.rsqrt(e[k, k])
            l = {m: e[m, k] * scale for m in range(k + 1, 8)}
            for m in range(k + 1, 8):
                for q in range(k + 1, m + 1):
                    e[m, q] = e[m, q] - l[m] * l[q]
            r[k] = r[k] * scale
            w[k] = w[k] * scale
            for m in range(k + 1, 8):
                r[m] = r[m] - l[m] * r[k]
                w[m] = w[m] - l[m] * w[k]
            for g in below:
                column = c[g, k] * scale
                for m in range(k + 1, 8):
                    c[g, m] = c[g, m] - l[m] * column
                new[g] = new[g] - column * w[k]
        u, v = r[0], w[0]
        for k in range(1, 8):
            u = jnp.where(sub == k, r[k], u)
            v = jnp.where(sub == k, w[k], v)
        u_ref[base : base + 8, :] = jnp.where(lane >= sub + base, u, 0.0)
        inv_ref[base : base + 8, :] = jnp.where(lane <= sub + base, v, 0.0)
        for g in below:
            rows[g] = new[g]


def factor_columns(a_ref, l_ref, hi_ref, lo_ref, col_ref, tile_ref, u_ref, inv_ref, begin, done):
    rows, order = l_ref.shape
    blocks = order // TILE

    def step(kb, carry):
        for b in range(blocks):

            @pl.when(kb == b)
            def _(b=b):
                at = b * TILE
                begin(b)
                col = a_ref[at:, at : at + TILE]
                if b:
                    left = (hi_ref[at:, :at], lo_ref[at:, :at])
                    right = (hi_ref[at : at + TILE, :at], lo_ref[at : at + TILE, :at])
                    col = col - dot3(left, right, NT)
                tile_ref[...] = col[:TILE]
                if at + TILE < rows:
                    col_ref[at + TILE :, :] = col[TILE:]

        factor_tile(tile_ref, u_ref, inv_ref)
        for b in range(blocks):

            @pl.when(kb == b)
            def _(b=b):
                at = b * TILE
                if b:
                    l_ref[:at, at : at + TILE] = jnp.zeros((at, TILE), F32)
                l_ref[at : at + TILE, at : at + TILE] = u_ref[...].T
                if at + TILE < rows:
                    panel = dot3(split(col_ref[at + TILE :, :]), split(inv_ref[...]), NT)
                    l_ref[at + TILE :, at : at + TILE] = panel
                    hi, lo = split(panel)
                    hi_ref[at + TILE :, at : at + TILE] = hi
                    lo_ref[at + TILE :, at : at + TILE] = lo
                done(b)

        return carry

    lax.fori_loop(0, blocks, step, 0)


def child_kernel(front, label, factor, share, a, row_c, col_c, l, hi, lo, col, tile, u, inv, in_sem, out_sem):
    loads = [
        pltpu.make_async_copy(
            front.at[:, b * TILE : (b + 1) * TILE], a.at[:, b * TILE : (b + 1) * TILE], in_sem.at[b]
        )
        for b in range(4)
    ]
    loads.append(pltpu.make_async_copy(front.at[K : K + PIECE, K : K + B], row_c, in_sem.at[4]))
    loads.append(pltpu.make_async_copy(front.at[K : K + B, K : K + PIECE], col_c, in_sem.at[5]))
    for load in loads:
        load.start()
    stores = [
        pltpu.make_async_copy(
            l.at[:, b * TILE : (b + 1) * TILE], factor.at[:, b * TILE : (b + 1) * TILE], out_sem.at[b]
        )
        for b in range(4)
    ]
    factor_columns(
        a, l, hi, lo, col, tile, u, inv, lambda b: loads[b].wait(), lambda b: stores[b].start()
    )
    loads[4].wait()
    loads[5].wait()
    head = (hi[K : K + PIECE, :], lo[K : K + PIECE, :])
    every = (hi[K:, :], lo[K:, :])
    row_c[...] = row_c[...] - dot3(head, every, NT)
    col_c[...] = col_c[...] - dot3(every, head, NT)
    for i in range(4):
        for j in range(4):
            s = 4 * i + j
            for h in range(2):
                at = i * PIECE + h * TILE + j * PANEL_OFF
                share[s, h * PANEL_OFF : (h + 1) * PANEL_OFF, :] = col_c[at : at + PANEL_OFF, :]
                at = h * TILE + i * PANEL_OFF
                share[s, (2 + h) * PANEL_OFF : (3 + h) * PANEL_OFF, :] = row_c[
                    at : at + PANEL_OFF, j * PIECE : (j + 1) * PIECE
                ]
                at = h * TILE + (4 * j + i) * CORNER_OFF
                to = 4 * PANEL_OFF + h * CORNER_OFF
                share[s, to : to + CORNER_OFF, :] = col_c[at : at + CORNER_OFF, :]
            share[s, LABEL_ROW:, :] = label[...]
    for store in stores:
        store.wait()


def child_call(front, label):
    order = front.shape[0]
    return pl.pallas_call(
        child_kernel,
        name="child_factor",
        in_specs=[ANY, VMEM],
        out_specs=[ANY, VMEM],
        out_shape=[
            jax.ShapeDtypeStruct((order, K), F32),
            jax.ShapeDtypeStruct((16, SHARE_ROWS, PIECE), F32),
        ],
        scratch_shapes=[
            pltpu.VMEM((order, K), F32),
            pltpu.VMEM((PIECE, B), F32),
            pltpu.VMEM((B, PIECE), F32),
            pltpu.VMEM((order, K), F32),
            pltpu.VMEM((order, K), BF16),
            pltpu.VMEM((order, K), BF16),
            pltpu.VMEM((order, TILE), F32),
            pltpu.VMEM((TILE, TILE), F32),
            pltpu.VMEM((TILE, TILE), F32),
            pltpu.VMEM((TILE, TILE), F32),
            pltpu.SemaphoreType.DMA((6,)),
            pltpu.SemaphoreType.DMA((4,)),
        ],
    )(front, label)


def update_kernel(here, panel, border, *refs):
    pieces, z = refs[:16], refs[16]
    part = split(panel[...])
    z[...] = border[...] - dot3(part, part, NT)
    for s in range(16):
        i = (here[1] + s // 4) & 3
        j = (here[2] + s % 4) & 3

        @pl.when((i > 0) & (j > 0))
        def _(s=s, i=i, j=j):
            t = pl.multiple_of((i - 1) * PIECE, PIECE)
            u = pl.multiple_of((j - 1) * PIECE, PIECE)
            pieces[s][...] = z[pl.ds(t, PIECE), pl.ds(u, PIECE)]


def update_call(here, front, factor):
    inner = B - PIECE
    at = front.shape[0] // inner - 1
    return pl.pallas_call(
        update_kernel,
        name="child_update",
        grid=(1,),
        in_specs=[
            SMEM,
            pl.BlockSpec((inner, K), lambda i: (at, 0)),
            pl.BlockSpec((inner, inner), lambda i: (at, at)),
        ],
        out_specs=[pl.BlockSpec((PIECE, PIECE), lambda i: (0, 0))] * 16,
        out_shape=[jax.ShapeDtypeStruct((PIECE, PIECE), F32)] * 16,
        scratch_shapes=[pltpu.VMEM((inner, inner), F32)],
    )(here, factor, front)


def regroup_kernel(labels, source, target, buffer, counts, in_sem, out_sem):
    for g in range(8):
        counts[g] = 0
    loads, stores = [], []
    for c in range(16):
        loads.append(pltpu.make_async_copy(source.at[c], buffer.at[c], in_sem.at[c]))
        loads[c].start()
    for c in range(16):
        g = labels[c, 8]
        slot = 2 * g + counts[g]
        counts[g] = counts[g] + 1
        loads[c].wait()
        stores.append(pltpu.make_async_copy(buffer.at[c], target.at[slot], out_sem.at[c]))
        stores[c].start()
    for c in range(16):
        stores[c].wait()


def regroup_call(labels, source):
    return pl.pallas_call(
        regroup_kernel,
        name="regroup",
        in_specs=[SMEM, ANY],
        out_specs=ANY,
        out_shape=jax.ShapeDtypeStruct(source.shape, source.dtype),
        scratch_shapes=[
            pltpu.VMEM(source.shape, source.dtype),
            pltpu.SMEM((8,), jnp.int32),
            pltpu.SemaphoreType.DMA((16,)),
            pltpu.SemaphoreType.DMA((16,)),
        ],
    )(labels, source)


def collect_kernel(here, labels, *refs):
    sources, target, buffer, counts, slots, in_sem, out_sem = refs[:16], *refs[16:]
    loads, stores = [], []
    for s in range(16):
        loads.append(pltpu.make_async_copy(sources[s], buffer.at[s], in_sem.at[s]))
        loads[s].start()
    for g in range(8):
        counts[g] = 0
    for c in range(16):
        g = labels[c, 8]
        slots[c] = 2 * g + counts[g]
        counts[g] = counts[g] + 1
    for s in range(16):
        c = 4 * ((here[1] + 4 - s // 4) & 3) + ((here[2] + 4 - s % 4) & 3)
        loads[s].wait()
        stores.append(pltpu.make_async_copy(buffer.at[s], target.at[slots[c]], out_sem.at[s]))
        stores[s].start()
    for s in range(16):
        stores[s].wait()


def collect_call(here, labels, sources):
    shape = (16, *sources[0].shape)
    return pl.pallas_call(
        collect_kernel,
        name="collect",
        in_specs=[SMEM, SMEM] + [ANY] * 16,
        out_specs=ANY,
        out_shape=jax.ShapeDtypeStruct(shape, F32),
        scratch_shapes=[
            pltpu.VMEM(shape, F32),
            pltpu.SMEM((8,), jnp.int32),
            pltpu.SMEM((16,), jnp.int32),
            pltpu.SemaphoreType.DMA((16,)),
            pltpu.SemaphoreType.DMA((16,)),
        ],
    )(here, labels, *sources)


def corner_split_kernel(here, p0, p1, p2, p3, o0, o1, o2, o3, buffer, sem):
    for q, part in enumerate((p0, p1, p2, p3)):

        @pl.when(here[2] == q)
        def _(part=part):
            copy = pltpu.make_async_copy(part, buffer, sem)
            copy.start()
            copy.wait()

    for r, out in enumerate((o0, o1, o2, o3)):
        out[...] = buffer[:, r * CORNER_OFF : (r + 1) * CORNER_OFF, :]


def corner_split_call(here, parts):
    out = jax.ShapeDtypeStruct((8, CORNER_OFF, B), F32)
    return pl.pallas_call(
        corner_split_kernel,
        name="corner_split",
        in_specs=[SMEM] + [ANY] * 4,
        out_specs=[VMEM] * 4,
        out_shape=[out] * 4,
        scratch_shapes=[pltpu.VMEM(parts[0].shape, F32), pltpu.SemaphoreType.DMA],
    )(here, *parts)


def share_kernel(here, kids, landed, *refs):
    row_e, col_e, corner_e = refs[:4], refs[4:8], refs[8:12]
    row_out, col_out, corner_out, corner, sem = refs[12:]
    row = here[1]
    col = here[2]
    for q in range(4):

        @pl.when(col == q)
        def _(q=q):
            copy = pltpu.make_async_copy(row_e[q], row_out, sem.at[0])
            copy.start()
            copy.wait()

        @pl.when(row == q)
        def _(q=q):
            first = pltpu.make_async_copy(col_e[q], col_out, sem.at[1])
            second = pltpu.make_async_copy(corner_e[q], corner, sem.at[2])
            first.start()
            second.start()
            first.wait()
            second.wait()

    for n, (t, u) in enumerate(LOWER):
        corner_out[n] = corner[t, :, u * TILE : (u + 1) * TILE]

    def add(n, carry):
        for h in range(2):
            for v in range(2):
                lanes = slice(v * TILE, (v + 1) * TILE)
                t = kids[n, 2 * row + h] - 8 * row
                u = pl.ds(pl.multiple_of(kids[n, v] * TILE, TILE), TILE)
                row_out[t, :, u] += landed[n, h * PANEL_OFF : (h + 1) * PANEL_OFF, lanes]
                t = kids[n, h]
                u = pl.ds(pl.multiple_of((kids[n, 2 * col + v] - 8 * col) * TILE, TILE), TILE)
                col_out[t, :, u] += landed[n, (2 + h) * PANEL_OFF : (3 + h) * PANEL_OFF, lanes]
                if v <= h:
                    at = 4 * PANEL_OFF + h * CORNER_OFF
                    index = lax.shift_right_logical(t * (t + 1), 1) + kids[n, v]
                    corner_out[index] += landed[n, at : at + CORNER_OFF, lanes]
        return carry

    lax.fori_loop(0, 16, add, 0)


def share_call(here, kids, landed, row_e, col_e, corner_e):
    panel = row_e[0].shape
    corner = (len(LOWER), CORNER_OFF, TILE)
    return pl.pallas_call(
        share_kernel,
        name="share_assembly",
        in_specs=[SMEM, SMEM, VMEM] + [ANY] * 12,
        out_specs=[VMEM] * 3,
        out_shape=[
            jax.ShapeDtypeStruct(panel, F32),
            jax.ShapeDtypeStruct(panel, F32),
            jax.ShapeDtypeStruct(corner, F32),
        ],
        scratch_shapes=[pltpu.VMEM(corner_e[0].shape, F32), pltpu.SemaphoreType.DMA((3,))],
    )(here, kids, landed, *row_e, *col_e, *corner_e)


def corner_kernel(parts, l, invs, a, hi, lo, col, tile, u, inv):
    for d in range(16):
        off = (4 * (d % 4) + d // 4) * CORNER_OFF
        for n, (t, v) in enumerate(LOWER):
            at = t * TILE + off
            a[at : at + CORNER_OFF, v * TILE : (v + 1) * TILE] = parts[d, n]

    def done(b):
        invs[b] = inv[...]

    factor_columns(a, l, hi, lo, col, tile, u, inv, lambda b: None, done)


def corner_call(parts):
    return pl.pallas_call(
        corner_kernel,
        name="corner_factor",
        in_specs=[VMEM],
        out_specs=[VMEM, VMEM],
        out_shape=[
            jax.ShapeDtypeStruct((E, E), F32),
            jax.ShapeDtypeStruct((E // TILE, TILE, TILE), F32),
        ],
        scratch_shapes=[
            pltpu.VMEM((E, E), F32),
            pltpu.VMEM((E, E), BF16),
            pltpu.VMEM((E, E), BF16),
            pltpu.VMEM((E, TILE), F32),
            pltpu.VMEM((TILE, TILE), F32),
            pltpu.VMEM((TILE, TILE), F32),
            pltpu.VMEM((TILE, TILE), F32),
        ],
    )(parts)


def solve_kernel(here, l, invs, *refs):
    row_parts, col_parts = refs[:4], refs[4:8]
    w, y, a, b, whi, wlo, yhi, ylo = refs[8:]
    for s in range(4):
        for target, parts, place in ((a, row_parts, here[2]), (b, col_parts, here[1])):
            off = ((place + 4 - s) & 3) * PANEL_OFF
            for t in range(8):
                at = pl.multiple_of(t * TILE + off, PANEL_OFF)
                target[pl.ds(at, PANEL_OFF), :] = parts[s][t]
    for k in range(E // TILE):
        at = k * TILE
        here = slice(at, at + TILE)
        inv = split(invs[k])
        left = a[:, here]
        right = b[here, :]
        if k:
            lower = split(l[here, :at])
            left = left - dot3((whi[:, :at], wlo[:, :at]), lower, NT)
            right = right - dot3(lower, (yhi[:at, :], ylo[:at, :]), NN)
        left = dot3(split(left), inv, NT)
        right = dot3(inv, split(right), NN)
        w[:, here] = left
        y[here, :] = right
        whi[:, here], wlo[:, here] = split(left)
        yhi[here, :], ylo[here, :] = split(right)


def solve_call(here, l, invs, row_parts, col_parts):
    return pl.pallas_call(
        solve_kernel,
        name="panel_solve",
        in_specs=[SMEM] + [VMEM] * 10,
        out_specs=[VMEM, VMEM],
        out_shape=[jax.ShapeDtypeStruct((B, E), F32), jax.ShapeDtypeStruct((E, B), F32)],
        scratch_shapes=[pltpu.VMEM((B, E), F32)] * 2 + [pltpu.VMEM((B, E), BF16)] * 4,
    )(here, l, invs, *row_parts, *col_parts)


def final_kernel(here, kids, entries, landed, l, w, y, out):
    row = here[1]
    col = here[2]

    @pl.when((row == 0) & (col == 0))
    def _():
        out[...] = l[...]

    @pl.when((row != 0) & (col == 0))
    def _():
        out[...] = w[...]

    @pl.when((row == 0) & (col != 0))
    def _():
        out[...] = y[...]

    @pl.when((row != 0) & (col != 0))
    def _():
        out[...] = entries[...] - dot3(split(w[...]), split(y[...]), NN)

        def add(n, carry):
            for h in range(2):
                for v in range(2):
                    t = (kids[n, 2 * row + h] - 8 * row) * TILE
                    u = (kids[n, 2 * col + v] - 8 * col) * TILE
                    out[pl.ds(pl.multiple_of(t, TILE), TILE), pl.ds(pl.multiple_of(u, TILE), TILE)] += (
                        landed[n, h * TILE : (h + 1) * TILE, v * TILE : (v + 1) * TILE]
                    )
            return carry

        lax.fori_loop(0, 16, add, 0)


def final_call(here, kids, entries, landed, l, w, y):
    return pl.pallas_call(
        final_kernel,
        name="trailing",
        in_specs=[SMEM, SMEM] + [VMEM] * 5,
        out_specs=VMEM,
        out_shape=jax.ShapeDtypeStruct(entries.shape, F32),
    )(here, kids, entries, landed, l, w, y)


def exchange(array, axes):
    return lax.all_to_all(array, axes, split_axis=0, concat_axis=0, tiled=True)


def shifts(array, axis):
    parts = [array]
    for s in range(1, 4):
        parts.append(lax.ppermute(array, axis, [(p, (p + s) % 4) for p in range(4)]))
    return parts


def from_first(parts, axis):
    out = [parts[0]]
    for q in range(1, 4):
        out.append(lax.ppermute(parts[q], axis, [(0, q)]))
    return out


def spread(pieces):
    out = [pieces[0]]
    for s in range(1, 16):
        perm = []
        for p in range(16):
            i = (p // 4 + s // 4) % 4
            j = (p % 4 + s % 4) % 4
            if i and j:
                perm.append((p, 4 * i + j))
        out.append(lax.ppermute(pieces[s], ("row", "col"), perm))
    return out


def program(child_fronts, parent_entries, tile_map, parent_group):
    plane = ("row", "col")
    front = child_fronts[0]
    entries = parent_entries[0]
    here = jnp.stack([lax.axis_index(name) for name in ("front", "row", "col")]).astype(jnp.int32)
    label = jnp.concatenate([tile_map[0], parent_group, jnp.zeros((PIECE - 9,), jnp.int32)])
    label = jnp.broadcast_to(label.astype(F32)[None], (8, PIECE))
    by_offset = entries.reshape(8, 4, PANEL_OFF, B)
    by_offset = [by_offset[:, q] for q in range(4)]
    row_e = from_first(by_offset, "col")
    col_e = from_first(by_offset, "row")
    factor, share = child_call(front, label)
    pieces = update_call(here, front, factor)
    corner_e = corner_split_call(here, row_e)
    corner_e = from_first(corner_e, "row")
    share_near = exchange(share, plane)
    labels = share_near[:, LABEL_ROW, :16].astype(jnp.int32)
    share_near = regroup_call(labels, share_near)
    share_far = exchange(share_near, "front")
    kids = share_far[:, LABEL_ROW, :8].astype(jnp.int32)
    pieces = spread(pieces)
    pieces_near = collect_call(here, labels, pieces)
    pieces_far = exchange(pieces_near, "front")
    row_own, col_own, corner_own = share_call(here, kids, share_far, row_e, col_e, corner_e)
    corner_parts = lax.all_gather(corner_own, plane)
    row_parts = shifts(row_own, "col")
    col_parts = shifts(col_own, "row")
    l, invs = corner_call(corner_parts)
    w, y = solve_call(here, l, invs, row_parts, col_parts)
    result = final_call(here, kids, entries, pieces_far, l, w, y)
    return (factor[None], result[None])


def solution(mesh):
    in_specs = (
        P(("front", "row", "col"), None, None),
        P("front", "row", "col"),
        P(("front", "row", "col"), None),
        P(("front", "row", "col")),
    )
    out_specs = (P(("front", "row", "col"), None, None), P("front", "row", "col"))
    return jax.shard_map(program, mesh=mesh, in_specs=in_specs, out_specs=out_specs, check_vma=False)
```

```python
import jax
import jax.numpy as jnp
from jax import lax
from jax.experimental import pallas as pl
from jax.experimental.pallas import tpu as pltpu
from jax.sharding import PartitionSpec as P


TILE = 128
F32 = jnp.float32
BF16 = jnp.bfloat16
VMEM = pl.BlockSpec(memory_space=pltpu.VMEM)
SMEM = pl.BlockSpec(memory_space=pltpu.SMEM)
ANY = pl.BlockSpec(memory_space=pl.ANY)
K = 512
B = 1024
E = 1024
N_COL = 4
PIECE = B // N_COL
CHUNK = 256
PANEL_OFF = TILE // N_COL
CORNER_OFF = TILE // (N_COL * N_COL)
LABEL_ROW = 4 * PANEL_OFF + 2 * CORNER_OFF
SHARE_ROWS = LABEL_ROW + 8
LOWER = [(t, u) for t in range(8) for u in range(t + 1)]


def split(x):
    hi = x.astype(BF16)
    return hi, (x - hi.astype(F32)).astype(BF16)


def dot3(a, b, dims):
    def one(x, y):
        return lax.dot_general(x, y, (dims, ((), ())), preferred_element_type=F32)

    return one(a[0], b[0]) + (one(a[0], b[1]) + one(a[1], b[0]))


NT = ((1,), (1,))
NN = ((1,), (0,))


def factor_tile(tile_ref, u_ref, inv_ref):
    count = TILE // 8
    lane = lax.broadcasted_iota(jnp.int32, (8, TILE), 1)
    sub = lax.broadcasted_iota(jnp.int32, (8, TILE), 0)
    rows = [tile_ref[8 * g : 8 * g + 8, :] for g in range(count)]

    def full(x):
        return jnp.broadcast_to(x, (8, TILE))

    for group in range(count):
        top = rows[group]
        base = 8 * group
        below = range(group + 1, count)
        lead = [full(top[:, base + k : base + k + 1]) for k in range(8)]
        e = {(m, k): full(lead[k][m : m + 1, :]) for k in range(8) for m in range(k, 8)}
        pivots = (lane >= base) & (lane < base + 8)
        unit = jnp.where(pivots, jnp.where(lane == sub + base, 1.0, 0.0), top)
        r = [full(top[k : k + 1, :]) for k in range(8)]
        w = [full(unit[k : k + 1, :]) for k in range(8)]
        fac = []
        for k in range(0, 8, 2):
            rest = range(k + 2, 8)
            a, b = e[k, k], e[k + 1, k]
            s0 = lax.rsqrt(a)
            rd = lax.rsqrt(a * e[k + 1, k + 1] - b * b)
            both = s0 * rd
            s1 = a * both
            l10 = b * s0
            l0 = {m: e[m, k] * s0 for m in rest}
            l1 = {m: (a * e[m, k + 1] - b * e[m, k]) * both for m in rest}
            for m in rest:
                for q in range(k + 2, m + 1):
                    e[m, q] = (e[m, q] - l0[m] * l0[q]) - l1[m] * l1[q]
            for x in (r, w):
                x[k] = x[k] * s0
                x[k + 1] = (x[k + 1] - l10 * x[k]) * s1
                for m in rest:
                    x[m] = (x[m] - l0[m] * x[k]) - l1[m] * x[k + 1]
            fac.append((s0, s1, l10, l0, l1))
        u, v = r[0], w[0]
        for k in range(1, 8):
            u = jnp.where(sub == k, r[k], u)
            v = jnp.where(sub == k, w[k], v)
        u_ref[base : base + 8, :] = jnp.where(lane >= sub + base, u, 0.0)
        inv_ref[base : base + 8, :] = jnp.where(lane <= sub + base, v, 0.0)
        for g in below:
            c = [full(rows[g][:, base + k : base + k + 1]) for k in range(8)]
            new = jnp.where(pivots, 0.0, rows[g])
            for k in range(0, 8, 2):
                s0, s1, l10, l0, l1 = fac[k // 2]
                c0 = c[k] * s0
                c1 = (c[k + 1] - l10 * c0) * s1
                for m in range(k + 2, 8):
                    c[m] = (c[m] - l0[m] * c0) - l1[m] * c1
                new = (new - c0 * w[k]) - c1 * w[k + 1]
            rows[g] = new


def factor_columns(a_ref, l_ref, hi_ref, lo_ref, col_ref, tile_ref, u_ref, inv_ref, begin, done):
    rows, order = l_ref.shape
    blocks = order // TILE

    def step(kb, carry):
        for b in range(blocks):

            @pl.when(kb == b)
            def _(b=b):
                at = b * TILE
                begin(b)
                col = a_ref[at:, at : at + TILE]
                if b:
                    left = (hi_ref[at:, :at], lo_ref[at:, :at])
                    right = (hi_ref[at : at + TILE, :at], lo_ref[at : at + TILE, :at])
                    col = col - dot3(left, right, NT)
                tile_ref[...] = col[:TILE]
                if at + TILE < rows:
                    col_ref[at + TILE :, :] = col[TILE:]

        factor_tile(tile_ref, u_ref, inv_ref)
        for b in range(blocks):

            @pl.when(kb == b)
            def _(b=b):
                at = b * TILE
                if b:
                    l_ref[:at, at : at + TILE] = jnp.zeros((at, TILE), F32)
                l_ref[at : at + TILE, at : at + TILE] = u_ref[...].T
                if at + TILE < rows:
                    panel = dot3(split(col_ref[at + TILE :, :]), split(inv_ref[...]), NT)
                    l_ref[at + TILE :, at : at + TILE] = panel
                    hi, lo = split(panel)
                    hi_ref[at + TILE :, at : at + TILE] = hi
                    lo_ref[at + TILE :, at : at + TILE] = lo
                done(b)

        return carry

    lax.fori_loop(0, blocks, step, 0)


def child_kernel(front, label, factor, share, a, row_c, col_c, l, hi, lo, col, tile, u, inv, in_sem, out_sem):
    loads = [
        pltpu.make_async_copy(
            front.at[:, b * TILE : (b + 1) * TILE], a.at[:, b * TILE : (b + 1) * TILE], in_sem.at[b]
        )
        for b in range(4)
    ]
    loads.append(pltpu.make_async_copy(front.at[K : K + PIECE, K : K + B], row_c, in_sem.at[4]))
    loads.append(pltpu.make_async_copy(front.at[K : K + B, K : K + PIECE], col_c, in_sem.at[5]))
    for load in loads:
        load.start()
    stores = [
        pltpu.make_async_copy(
            l.at[:, b * TILE : (b + 1) * TILE], factor.at[:, b * TILE : (b + 1) * TILE], out_sem.at[b]
        )
        for b in range(4)
    ]
    factor_columns(
        a, l, hi, lo, col, tile, u, inv, lambda b: loads[b].wait(), lambda b: stores[b].start()
    )
    loads[4].wait()
    loads[5].wait()
    head = (hi[K : K + PIECE, :], lo[K : K + PIECE, :])
    every = (hi[K:, :], lo[K:, :])
    row_c[...] = row_c[...] - dot3(head, every, NT)
    col_c[...] = col_c[...] - dot3(every, head, NT)
    for i in range(4):
        for j in range(4):
            s = 4 * i + j
            for h in range(2):
                at = i * PIECE + h * TILE + j * PANEL_OFF
                share[s, h * PANEL_OFF : (h + 1) * PANEL_OFF, :] = col_c[at : at + PANEL_OFF, :]
                at = h * TILE + i * PANEL_OFF
                share[s, (2 + h) * PANEL_OFF : (3 + h) * PANEL_OFF, :] = row_c[
                    at : at + PANEL_OFF, j * PIECE : (j + 1) * PIECE
                ]
                at = h * TILE + (4 * j + i) * CORNER_OFF
                to = 4 * PANEL_OFF + h * CORNER_OFF
                share[s, to : to + CORNER_OFF, :] = col_c[at : at + CORNER_OFF, :]
            share[s, LABEL_ROW:, :] = label[...]
    for store in stores:
        store.wait()


def child_call(front, label):
    order = front.shape[0]
    return pl.pallas_call(
        child_kernel,
        name="child_factor",
        in_specs=[ANY, VMEM],
        out_specs=[ANY, VMEM],
        out_shape=[
            jax.ShapeDtypeStruct((order, K), F32),
            jax.ShapeDtypeStruct((16, SHARE_ROWS, PIECE), F32),
        ],
        scratch_shapes=[
            pltpu.VMEM((order, K), F32),
            pltpu.VMEM((PIECE, B), F32),
            pltpu.VMEM((B, PIECE), F32),
            pltpu.VMEM((order, K), F32),
            pltpu.VMEM((order, K), BF16),
            pltpu.VMEM((order, K), BF16),
            pltpu.VMEM((order, TILE), F32),
            pltpu.VMEM((TILE, TILE), F32),
            pltpu.VMEM((TILE, TILE), F32),
            pltpu.VMEM((TILE, TILE), F32),
            pltpu.SemaphoreType.DMA((6,)),
            pltpu.SemaphoreType.DMA((4,)),
        ],
    )(front, label)


def update_kernel(panel, border, pieces):
    part = split(panel[...])
    z = border[...] - dot3(part, part, NT)
    for i in range(3):
        for j in range(3):
            pieces[4 * (i + 1) + j + 1] = z[
                i * PIECE : (i + 1) * PIECE, j * PIECE : (j + 1) * PIECE
            ]


def update_call(front, factor):
    inner = B - PIECE
    at = front.shape[0] // inner - 1
    return pl.pallas_call(
        update_kernel,
        name="child_update",
        grid=(1,),
        in_specs=[
            pl.BlockSpec((inner, K), lambda i: (at, 0)),
            pl.BlockSpec((inner, inner), lambda i: (at, at)),
        ],
        out_specs=pl.BlockSpec((16, PIECE, PIECE), lambda i: (0, 0, 0)),
        out_shape=jax.ShapeDtypeStruct((16, PIECE, PIECE), F32),
    )(factor, front)


def regroup_kernel(labels, source, target, buffer, counts, in_sem, out_sem):
    for g in range(8):
        counts[g] = 0
    loads, stores = [], []
    for c in range(16):
        loads.append(pltpu.make_async_copy(source.at[c], buffer.at[c], in_sem.at[c]))
        loads[c].start()
    for c in range(16):
        g = labels[c, 8]
        slot = 2 * g + counts[g]
        counts[g] = counts[g] + 1
        loads[c].wait()
        stores.append(pltpu.make_async_copy(buffer.at[c], target.at[slot], out_sem.at[c]))
        stores[c].start()
    for c in range(16):
        stores[c].wait()


def regroup_call(labels, source):
    return pl.pallas_call(
        regroup_kernel,
        name="regroup",
        in_specs=[SMEM, ANY],
        out_specs=ANY,
        out_shape=jax.ShapeDtypeStruct(source.shape, source.dtype),
        scratch_shapes=[
            pltpu.VMEM(source.shape, source.dtype),
            pltpu.SMEM((8,), jnp.int32),
            pltpu.SemaphoreType.DMA((16,)),
            pltpu.SemaphoreType.DMA((16,)),
        ],
    )(labels, source)


def deal_kernel(here, labels, source, *refs):
    targets, (buffer, counts, in_sem, out_sem) = refs[:8], refs[8:]
    for g in range(8):
        counts[g] = 0
    loads = []
    for c in range(16):
        g = labels[c, 8]
        d = (g + 8 - here[0]) & 7
        loads.append(pltpu.make_async_copy(source.at[c], buffer.at[d, counts[g]], in_sem.at[c]))
        counts[g] = counts[g] + 1
        loads[c].start()
    for load in loads:
        load.wait()
    stores = [
        pltpu.make_async_copy(buffer.at[d], targets[d], out_sem.at[d]) for d in range(8)
    ]
    for store in stores:
        store.start()
    for store in stores:
        store.wait()


def deal_call(here, labels, source):
    shape = (2, *source.shape[1:])
    return pl.pallas_call(
        deal_kernel,
        name="deal",
        in_specs=[SMEM, SMEM, ANY],
        out_specs=[ANY] * 8,
        out_shape=[jax.ShapeDtypeStruct(shape, F32)] * 8,
        scratch_shapes=[
            pltpu.VMEM((8, *shape), F32),
            pltpu.SMEM((8,), jnp.int32),
            pltpu.SemaphoreType.DMA((16,)),
            pltpu.SemaphoreType.DMA((8,)),
        ],
    )(here, labels, source)


def pack_kernel(here, entries, o0, o1, o2, sem):
    row = here[1]
    col = here[2]

    @pl.when((row == 0) | (col == 0))
    def _():
        copies = []
        for s, out in enumerate((o0, o1, o2)):
            by_row = 1 + lax.rem(row + 2 + s, 3)
            by_col = 1 + lax.rem(col + 4 - s, 3)
            q = jnp.where(row == 0, jnp.where(col == 0, 1 + s, by_col), by_row)
            copies.append(pltpu.make_async_copy(entries.at[:, q], out, sem.at[s]))
            copies[s].start()
        for copy in copies:
            copy.wait()


def pack_call(here, entries):
    out = jax.ShapeDtypeStruct((8, PANEL_OFF, B), F32)
    return pl.pallas_call(
        pack_kernel,
        name="pack",
        in_specs=[SMEM, ANY],
        out_specs=[VMEM] * 3,
        out_shape=[out] * 3,
        scratch_shapes=[pltpu.SemaphoreType.DMA((3,))],
    )(here, entries)


def pick_start(use, sources, target, sem):
    for q, source in enumerate(sources):

        @pl.when(use == q)
        def _(source=source):
            pltpu.make_async_copy(source, target, sem).start()

    return pltpu.make_async_copy(sources[-1], target, sem)


def corner_split_kernel(here, entries, p0, p1, p2, o0, o1, o2, o3, buffer, sem):
    pick_start(here[2], (entries.at[:, 0], p0, p1, p2), buffer, sem).wait()
    for r, out in enumerate((o0, o1, o2, o3)):
        out[...] = buffer[:, r * CORNER_OFF : (r + 1) * CORNER_OFF, :]


def corner_split_call(here, entries, parts):
    out = jax.ShapeDtypeStruct((8, CORNER_OFF, B), F32)
    return pl.pallas_call(
        corner_split_kernel,
        name="corner_split",
        in_specs=[SMEM] + [ANY] * 4,
        out_specs=[VMEM] * 4,
        out_shape=[out] * 4,
        scratch_shapes=[pltpu.VMEM(parts[0].shape, F32), pltpu.SemaphoreType.DMA],
    )(here, entries, *parts)


def share_kernel(here, kids, entries, *refs):
    parts, corner_e, landed = refs[:3], refs[3:7], refs[7:15]
    row_out, col_out, corner_out, corner, sem = refs[15:]
    row = here[1]
    col = here[2]
    sources = (entries.at[:, 0], *parts)
    from_row = jnp.where(col == 0, 0, 1 + lax.rem(col + 3 - row, 3))
    from_col = jnp.where(row == 0, 0, 1 + lax.rem(col + 5 - row, 3))
    picks = (
        pick_start(from_row, sources, row_out, sem.at[0]),
        pick_start(from_col, sources, col_out, sem.at[1]),
        pick_start(row, corner_e, corner, sem.at[2]),
    )
    for pick in picks:
        pick.wait()
    for n, (t, u) in enumerate(LOWER):
        corner_out[n] = corner[t, :, u * TILE : (u + 1) * TILE]

    for d in range(8):
        add_share(row, col, kids, landed[d], 2 * d, row_out, col_out, corner_out)


def add_share(row, col, kids, landed, begin, row_out, col_out, corner_out):
    def add(at_piece, carry):
        n = begin + at_piece
        for h in range(2):
            for v in range(2):
                lanes = slice(v * TILE, (v + 1) * TILE)
                t = kids[n, 2 * row + h] - 8 * row
                u = pl.ds(pl.multiple_of(kids[n, v] * TILE, TILE), TILE)
                row_out[t, :, u] += landed[at_piece, h * PANEL_OFF : (h + 1) * PANEL_OFF, lanes]
                t = kids[n, h]
                u = pl.ds(pl.multiple_of((kids[n, 2 * col + v] - 8 * col) * TILE, TILE), TILE)
                col_out[t, :, u] += landed[at_piece, (2 + h) * PANEL_OFF : (3 + h) * PANEL_OFF, lanes]
                if v <= h:
                    at = 4 * PANEL_OFF + h * CORNER_OFF
                    index = lax.shift_right_logical(t * (t + 1), 1) + kids[n, v]
                    corner_out[index] += landed[at_piece, at : at + CORNER_OFF, lanes]
        return carry

    lax.fori_loop(0, 2, add, 0)


def share_call(here, kids, entries, parts, corner_e, landed):
    panel = parts[0].shape
    corner = (len(LOWER), CORNER_OFF, TILE)
    return pl.pallas_call(
        share_kernel,
        name="share_assembly",
        in_specs=[SMEM, SMEM] + [ANY] * 8 + [VMEM] * 8,
        out_specs=[VMEM] * 3,
        out_shape=[
            jax.ShapeDtypeStruct(panel, F32),
            jax.ShapeDtypeStruct(panel, F32),
            jax.ShapeDtypeStruct(corner, F32),
        ],
        scratch_shapes=[pltpu.VMEM(corner_e[0].shape, F32), pltpu.SemaphoreType.DMA((3,))],
    )(here, kids, entries, *parts, *corner_e, *landed)


def corner_kernel(parts, l, invs, a, hi, lo, col, tile, u, inv):
    for d in range(16):
        off = (4 * (d % 4) + d // 4) * CORNER_OFF
        for n, (t, v) in enumerate(LOWER):
            at = t * TILE + off
            a[at : at + CORNER_OFF, v * TILE : (v + 1) * TILE] = parts[d, n]

    def done(b):
        invs[b] = inv[...]

    factor_columns(a, l, hi, lo, col, tile, u, inv, lambda b: None, done)


def corner_call(parts):
    return pl.pallas_call(
        corner_kernel,
        name="corner_factor",
        in_specs=[VMEM],
        out_specs=[VMEM, VMEM],
        out_shape=[
            jax.ShapeDtypeStruct((E, E), F32),
            jax.ShapeDtypeStruct((E // TILE, TILE, TILE), F32),
        ],
        scratch_shapes=[
            pltpu.VMEM((E, E), F32),
            pltpu.VMEM((E, E), BF16),
            pltpu.VMEM((E, E), BF16),
            pltpu.VMEM((E, TILE), F32),
            pltpu.VMEM((TILE, TILE), F32),
            pltpu.VMEM((TILE, TILE), F32),
            pltpu.VMEM((TILE, TILE), F32),
        ],
    )(parts)


def copy_rows(source, target):
    def chunk(c, carry):
        part = pl.ds(pl.multiple_of(c * TILE, TILE), TILE)
        target[part, :] = source[part, :]
        return carry

    lax.fori_loop(0, source.shape[0] // TILE, chunk, 0)


def parent_kernel(here, kids, l, invs, *refs):
    row_parts, col_parts = refs[:4], refs[4:8]
    entries, landed, out, a, b, whi, wlo, yhi, ylo, block, pieces, sem = refs[8:]
    row = here[1]
    col = here[2]
    loads = (
        pltpu.make_async_copy(entries, block, sem.at[0]),
        pltpu.make_async_copy(landed, pieces, sem.at[1]),
    )
    for load in loads:
        load.start()

    def arrange(t, carry):
        for s in range(4):
            for target, parts, place in ((a, row_parts, col), (b, col_parts, row)):
                at = t * TILE + ((place + 4 - s) & 3) * PANEL_OFF
                target[pl.ds(pl.multiple_of(at, PANEL_OFF), PANEL_OFF), :] = parts[s][t]
        return carry

    lax.fori_loop(0, 8, arrange, 0)
    wide = 2 * TILE
    for k in range(E // wide):
        at = k * wide
        mid = at + TILE
        here_k = slice(at, at + wide)
        first = split(invs[2 * k])
        second = split(invs[2 * k + 1])
        below = split(dot3(second, split(l[mid : at + wide, at:mid]), NN))
        below = -dot3(below, first, NN)
        zero = jnp.zeros((TILE, TILE), F32)
        inv = split(
            jnp.concatenate(
                [
                    jnp.concatenate([invs[2 * k], zero], 1),
                    jnp.concatenate([below, invs[2 * k + 1]], 1),
                ],
                0,
            )
        )
        lower = split(l[here_k, :at]) if k else None

        def chunk(c, carry):
            part = pl.ds(pl.multiple_of(c * CHUNK, CHUNK), CHUNK)
            left = a[part, here_k]
            right = b[here_k, part]
            if k:
                left = left - dot3((whi[part, :at], wlo[part, :at]), lower, NT)
                right = right - dot3(lower, (yhi[:at, part], ylo[:at, part]), NN)
            left = dot3(split(left), inv, NT)
            right = dot3(inv, split(right), NN)
            a[part, here_k] = left
            b[here_k, part] = right
            whi[part, here_k], wlo[part, here_k] = split(left)
            yhi[here_k, part], ylo[here_k, part] = split(right)
            return carry

        lax.fori_loop(0, B // CHUNK, chunk, 0)
    for load in loads:
        load.wait()

    @pl.when((row == 0) & (col == 0))
    def _():
        copy_rows(l, out)

    @pl.when((row != 0) & (col == 0))
    def _():
        copy_rows(a, out)

    @pl.when((row == 0) & (col != 0))
    def _():
        copy_rows(b, out)

    @pl.when((row != 0) & (col != 0))
    def _():
        def chunk(c, carry):
            part = pl.ds(pl.multiple_of(c * CHUNK, CHUNK), CHUNK)
            right = (yhi[...], ylo[...])
            out[part, :] = block[part, :] - dot3((whi[part, :], wlo[part, :]), right, NN)
            return carry

        lax.fori_loop(0, B // CHUNK, chunk, 0)

        def add(n, carry):
            plane = lax.shift_right_logical(n, 1)
            child = 2 * ((here[0] + 8 - plane) & 7) + (n & 1)
            for h in range(2):
                for v in range(2):
                    t = pl.multiple_of((kids[child, 2 * row + h] - 8 * row) * TILE, TILE)
                    u = pl.multiple_of((kids[child, 2 * col + v] - 8 * col) * TILE, TILE)
                    out[pl.ds(t, TILE), pl.ds(u, TILE)] += pieces[
                        n, h * TILE : (h + 1) * TILE, v * TILE : (v + 1) * TILE
                    ]
            return carry

        lax.fori_loop(0, 16, add, 0)


def parent_call(here, kids, l, invs, row_parts, col_parts, entries, landed):
    return pl.pallas_call(
        parent_kernel,
        name="parent",
        in_specs=[SMEM, SMEM] + [VMEM] * 10 + [ANY] * 2,
        out_specs=VMEM,
        out_shape=jax.ShapeDtypeStruct((B, B), F32),
        scratch_shapes=[pltpu.VMEM((B, E), F32)] * 2
        + [pltpu.VMEM((B, E), BF16)] * 4
        + [
            pltpu.VMEM((B, B), F32),
            pltpu.VMEM(landed.shape, F32),
            pltpu.SemaphoreType.DMA((2,)),
        ],
    )(here, kids, l, invs, *row_parts, *col_parts, entries, landed)


def exchange(array, axes):
    return lax.all_to_all(array, axes, split_axis=0, concat_axis=0, tiled=True)


def shifts(array, axis):
    parts = [array]
    for s in range(1, 4):
        parts.append(lax.ppermute(array, axis, [(p, (p + s) % 4) for p in range(4)]))
    return parts


def hand_out(packed):
    out = []
    for s in range(3):
        perm = [(0, 1 + s)]
        for i in range(3):
            perm.append((4 * (1 + i), 4 * (1 + i) + 1 + (i + s) % 3))
            perm.append((1 + i, 4 * (1 + (i - s - 1) % 3) + 1 + i))
        out.append(lax.ppermute(packed[s], ("row", "col"), perm))
    return out


def from_first(parts, axis):
    out = [parts[0]]
    for q in range(1, 4):
        out.append(lax.ppermute(parts[q], axis, [(0, q)]))
    return out


def program(child_fronts, parent_entries, tile_map, parent_group):
    plane = ("row", "col")
    front = child_fronts[0]
    entries = parent_entries[0]
    here = jnp.stack([lax.axis_index(name) for name in ("front", "row", "col")]).astype(jnp.int32)
    label = jnp.concatenate([tile_map[0], parent_group, jnp.zeros((PIECE - 9,), jnp.int32)])
    label = jnp.broadcast_to(label.astype(F32)[None], (8, PIECE))
    by_offset = entries.reshape(8, 4, PANEL_OFF, B)
    packed = pack_call(here, by_offset)
    parts_e = hand_out(packed)
    factor, share = child_call(front, label)
    pieces = update_call(front, factor)
    share_near = exchange(share, plane)
    corner_e = corner_split_call(here, by_offset, parts_e)
    corner_e = from_first(corner_e, "row")
    labels = share_near[:, LABEL_ROW, :16].astype(jnp.int32)
    dealt = deal_call(here, labels, share_near)
    landed = [dealt[0]]
    for d in range(1, 8):
        landed.append(lax.ppermute(dealt[d], "front", [(f, (f + d) % 8) for f in range(8)]))
    kids = jnp.concatenate([part[:, LABEL_ROW, :8] for part in landed]).astype(jnp.int32)
    pieces_near = exchange(pieces, plane)
    pieces_near = regroup_call(labels, pieces_near)
    pieces_far = exchange(pieces_near, "front")
    row_own, col_own, corner_own = share_call(here, kids, by_offset, parts_e, corner_e, landed)
    corner_parts = lax.all_gather(corner_own, plane)
    row_parts = shifts(row_own, "col")
    col_parts = shifts(col_own, "row")
    l, invs = corner_call(corner_parts)
    result = parent_call(here, kids, l, invs, row_parts, col_parts, entries, pieces_far)
    return (factor[None], result[None])


def solution(mesh):
    in_specs = (
        P(("front", "row", "col"), None, None),
        P("front", "row", "col"),
        P(("front", "row", "col"), None),
        P(("front", "row", "col")),
    )
    out_specs = (P(("front", "row", "col"), None, None), P("front", "row", "col"))
    return jax.shard_map(program, mesh=mesh, in_specs=in_specs, out_specs=out_specs, check_vma=False)
```

```python
import jax
import jax.numpy as jnp
from jax import lax
from jax.experimental import pallas as pl
from jax.experimental.pallas import tpu as pltpu
from jax.sharding import PartitionSpec as P


TILE = 128
F32 = jnp.float32
BF16 = jnp.bfloat16
VMEM = pl.BlockSpec(memory_space=pltpu.VMEM)
SMEM = pl.BlockSpec(memory_space=pltpu.SMEM)
ANY = pl.BlockSpec(memory_space=pl.ANY)
K = 512
B = 1024
E = 1024
N_COL = 4
PIECE = B // N_COL
CHUNK = 256
PANEL_OFF = TILE // N_COL
CORNER_OFF = TILE // (N_COL * N_COL)
LABEL_ROW = 4 * PANEL_OFF + 2 * CORNER_OFF
SHARE_ROWS = LABEL_ROW + 8
LOWER = [(t, u) for t in range(8) for u in range(t + 1)]


def split(x):
    hi = x.astype(BF16)
    return hi, (x - hi.astype(F32)).astype(BF16)


def dot3(a, b, dims):
    def one(x, y):
        return lax.dot_general(x, y, (dims, ((), ())), preferred_element_type=F32)

    return one(a[0], b[0]) + (one(a[0], b[1]) + one(a[1], b[0]))


NT = ((1,), (1,))
NN = ((1,), (0,))


def factor_tile(tile_ref, u_ref, inv_ref):
    count = TILE // 8
    lane = lax.broadcasted_iota(jnp.int32, (8, TILE), 1)
    sub = lax.broadcasted_iota(jnp.int32, (8, TILE), 0)
    rows = [tile_ref[8 * g : 8 * g + 8, :] for g in range(count)]

    def full(x):
        return jnp.broadcast_to(x, (8, TILE))

    for group in range(count):
        top = rows[group]
        base = 8 * group
        below = range(group + 1, count)
        lead = [full(top[:, base + k : base + k + 1]) for k in range(8)]
        e = {(m, k): full(lead[k][m : m + 1, :]) for k in range(8) for m in range(k, 8)}
        pivots = (lane >= base) & (lane < base + 8)
        unit = jnp.where(pivots, jnp.where(lane == sub + base, 1.0, 0.0), top)
        r = [full(top[k : k + 1, :]) for k in range(8)]
        w = [full(unit[k : k + 1, :]) for k in range(8)]
        fac = []
        for k in range(0, 8, 2):
            rest = range(k + 2, 8)
            a, b = e[k, k], e[k + 1, k]
            s0 = lax.rsqrt(a)
            rd = lax.rsqrt(a * e[k + 1, k + 1] - b * b)
            both = s0 * rd
            s1 = a * both
            l10 = b * s0
            l0 = {m: e[m, k] * s0 for m in rest}
            l1 = {m: (a * e[m, k + 1] - b * e[m, k]) * both for m in rest}
            for m in rest:
                for q in range(k + 2, m + 1):
                    e[m, q] = (e[m, q] - l0[m] * l0[q]) - l1[m] * l1[q]
            for x in (r, w):
                x[k] = x[k] * s0
                x[k + 1] = (x[k + 1] - l10 * x[k]) * s1
                for m in rest:
                    x[m] = (x[m] - l0[m] * x[k]) - l1[m] * x[k + 1]
            fac.append((s0, s1, l10, l0, l1))
        u, v = r[0], w[0]
        for k in range(1, 8):
            u = jnp.where(sub == k, r[k], u)
            v = jnp.where(sub == k, w[k], v)
        u_ref[base : base + 8, :] = jnp.where(lane >= sub + base, u, 0.0)
        inv_ref[base : base + 8, :] = jnp.where(lane <= sub + base, v, 0.0)
        for g in below:
            c = [full(rows[g][:, base + k : base + k + 1]) for k in range(8)]
            new = jnp.where(pivots, 0.0, rows[g])
            for k in range(0, 8, 2):
                s0, s1, l10, l0, l1 = fac[k // 2]
                c0 = c[k] * s0
                c1 = (c[k + 1] - l10 * c0) * s1
                for m in range(k + 2, 8):
                    c[m] = (c[m] - l0[m] * c0) - l1[m] * c1
                new = (new - c0 * w[k]) - c1 * w[k + 1]
            rows[g] = new


def factor_columns(a_ref, l_ref, hi_ref, lo_ref, col_ref, tile_ref, u_ref, inv_ref, begin, done):
    rows, order = l_ref.shape
    blocks = order // TILE

    def step(kb, carry):
        for b in range(blocks):

            @pl.when(kb == b)
            def _(b=b):
                at = b * TILE
                begin(b)
                col = a_ref[at:, at : at + TILE]
                if b:
                    left = (hi_ref[at:, :at], lo_ref[at:, :at])
                    right = (hi_ref[at : at + TILE, :at], lo_ref[at : at + TILE, :at])
                    col = col - dot3(left, right, NT)
                tile_ref[...] = col[:TILE]
                if at + TILE < rows:
                    col_ref[at + TILE :, :] = col[TILE:]

        factor_tile(tile_ref, u_ref, inv_ref)
        for b in range(blocks):

            @pl.when(kb == b)
            def _(b=b):
                at = b * TILE
                if b:
                    l_ref[:at, at : at + TILE] = jnp.zeros((at, TILE), F32)
                l_ref[at : at + TILE, at : at + TILE] = u_ref[...].T
                if at + TILE < rows:
                    panel = dot3(split(col_ref[at + TILE :, :]), split(inv_ref[...]), NT)
                    l_ref[at + TILE :, at : at + TILE] = panel
                    hi, lo = split(panel)
                    hi_ref[at + TILE :, at : at + TILE] = hi
                    lo_ref[at + TILE :, at : at + TILE] = lo
                done(b)

        return carry

    lax.fori_loop(0, blocks, step, 0)


def child_kernel(front, label, factor, share, a, row_c, col_c, l, hi, lo, col, tile, u, inv, in_sem, out_sem):
    loads = [
        pltpu.make_async_copy(
            front.at[:, b * TILE : (b + 1) * TILE], a.at[:, b * TILE : (b + 1) * TILE], in_sem.at[b]
        )
        for b in range(4)
    ]
    loads.append(pltpu.make_async_copy(front.at[K : K + PIECE, K : K + B], row_c, in_sem.at[4]))
    loads.append(pltpu.make_async_copy(front.at[K : K + B, K : K + PIECE], col_c, in_sem.at[5]))
    for load in loads:
        load.start()
    stores = [
        pltpu.make_async_copy(
            l.at[:, b * TILE : (b + 1) * TILE], factor.at[:, b * TILE : (b + 1) * TILE], out_sem.at[b]
        )
        for b in range(4)
    ]
    factor_columns(
        a, l, hi, lo, col, tile, u, inv, lambda b: loads[b].wait(), lambda b: stores[b].start()
    )
    loads[4].wait()
    loads[5].wait()
    head = (hi[K : K + PIECE, :], lo[K : K + PIECE, :])
    every = (hi[K:, :], lo[K:, :])
    row_c[...] = row_c[...] - dot3(head, every, NT)
    col_c[...] = col_c[...] - dot3(every, head, NT)
    for i in range(4):
        for j in range(4):
            s = 4 * i + j
            for h in range(2):
                at = i * PIECE + h * TILE + j * PANEL_OFF
                share[s, h * PANEL_OFF : (h + 1) * PANEL_OFF, :] = col_c[at : at + PANEL_OFF, :]
                at = h * TILE + i * PANEL_OFF
                share[s, (2 + h) * PANEL_OFF : (3 + h) * PANEL_OFF, :] = row_c[
                    at : at + PANEL_OFF, j * PIECE : (j + 1) * PIECE
                ]
                at = h * TILE + (4 * j + i) * CORNER_OFF
                to = 4 * PANEL_OFF + h * CORNER_OFF
                share[s, to : to + CORNER_OFF, :] = col_c[at : at + CORNER_OFF, :]
            share[s, LABEL_ROW:, :] = label[...]
    for store in stores:
        store.wait()


def child_call(front, label):
    order = front.shape[0]
    return pl.pallas_call(
        child_kernel,
        name="child_factor",
        in_specs=[ANY, VMEM],
        out_specs=[ANY, VMEM],
        out_shape=[
            jax.ShapeDtypeStruct((order, K), F32),
            jax.ShapeDtypeStruct((16, SHARE_ROWS, PIECE), F32),
        ],
        scratch_shapes=[
            pltpu.VMEM((order, K), F32),
            pltpu.VMEM((PIECE, B), F32),
            pltpu.VMEM((B, PIECE), F32),
            pltpu.VMEM((order, K), F32),
            pltpu.VMEM((order, K), BF16),
            pltpu.VMEM((order, K), BF16),
            pltpu.VMEM((order, TILE), F32),
            pltpu.VMEM((TILE, TILE), F32),
            pltpu.VMEM((TILE, TILE), F32),
            pltpu.VMEM((TILE, TILE), F32),
            pltpu.SemaphoreType.DMA((6,)),
            pltpu.SemaphoreType.DMA((4,)),
        ],
    )(front, label)


def update_kernel(panel, border, pieces):
    part = split(panel[...])
    z = border[...] - dot3(part, part, NT)
    for i in range(3):
        for j in range(3):
            pieces[4 * (i + 1) + j + 1] = z[
                i * PIECE : (i + 1) * PIECE, j * PIECE : (j + 1) * PIECE
            ]


def update_call(front, factor):
    inner = B - PIECE
    at = front.shape[0] // inner - 1
    return pl.pallas_call(
        update_kernel,
        name="child_update",
        grid=(1,),
        in_specs=[
            pl.BlockSpec((inner, K), lambda i: (at, 0)),
            pl.BlockSpec((inner, inner), lambda i: (at, at)),
        ],
        out_specs=pl.BlockSpec((16, PIECE, PIECE), lambda i: (0, 0, 0)),
        out_shape=jax.ShapeDtypeStruct((16, PIECE, PIECE), F32),
    )(factor, front)


def regroup_kernel(labels, source, target, buffer, counts, in_sem, out_sem):
    for g in range(8):
        counts[g] = 0
    loads, stores = [], []
    for c in range(16):
        loads.append(pltpu.make_async_copy(source.at[c], buffer.at[c], in_sem.at[c]))
        loads[c].start()
    for c in range(16):
        g = labels[c, 8]
        slot = 2 * g + counts[g]
        counts[g] = counts[g] + 1
        loads[c].wait()
        stores.append(pltpu.make_async_copy(buffer.at[c], target.at[slot], out_sem.at[c]))
        stores[c].start()
    for c in range(16):
        stores[c].wait()


def regroup_call(labels, source):
    return pl.pallas_call(
        regroup_kernel,
        name="regroup",
        in_specs=[SMEM, ANY],
        out_specs=ANY,
        out_shape=jax.ShapeDtypeStruct(source.shape, source.dtype),
        scratch_shapes=[
            pltpu.VMEM(source.shape, source.dtype),
            pltpu.SMEM((8,), jnp.int32),
            pltpu.SemaphoreType.DMA((16,)),
            pltpu.SemaphoreType.DMA((16,)),
        ],
    )(labels, source)


def deal_kernel(here, labels, source, *refs):
    targets, (buffer, counts, in_sem, out_sem) = refs[:8], refs[8:]
    for g in range(8):
        counts[g] = 0
    loads = []
    for c in range(16):
        g = labels[c, 8]
        d = (g + 8 - here[0]) & 7
        loads.append(pltpu.make_async_copy(source.at[c], buffer.at[d, counts[g]], in_sem.at[c]))
        counts[g] = counts[g] + 1
        loads[c].start()
    for load in loads:
        load.wait()
    stores = [
        pltpu.make_async_copy(buffer.at[d], targets[d], out_sem.at[d]) for d in range(8)
    ]
    for store in stores:
        store.start()
    for store in stores:
        store.wait()


def deal_call(here, labels, source):
    shape = (2, *source.shape[1:])
    return pl.pallas_call(
        deal_kernel,
        name="deal",
        in_specs=[SMEM, SMEM, ANY],
        out_specs=[ANY] * 8,
        out_shape=[jax.ShapeDtypeStruct(shape, F32)] * 8,
        scratch_shapes=[
            pltpu.VMEM((8, *shape), F32),
            pltpu.SMEM((8,), jnp.int32),
            pltpu.SemaphoreType.DMA((16,)),
            pltpu.SemaphoreType.DMA((8,)),
        ],
    )(here, labels, source)


def pack_kernel(here, entries, o0, o1, o2, sem):
    row = here[1]
    col = here[2]

    @pl.when((row == 0) | (col == 0))
    def _():
        copies = []
        for s, out in enumerate((o0, o1, o2)):
            by_row = 1 + lax.rem(row + 2 + s, 3)
            by_col = 1 + lax.rem(col + 4 - s, 3)
            q = jnp.where(row == 0, jnp.where(col == 0, 1 + s, by_col), by_row)
            copies.append(pltpu.make_async_copy(entries.at[:, q], out, sem.at[s]))
            copies[s].start()
        for copy in copies:
            copy.wait()


def pack_call(here, entries):
    out = jax.ShapeDtypeStruct((8, PANEL_OFF, B), F32)
    return pl.pallas_call(
        pack_kernel,
        name="pack",
        in_specs=[SMEM, ANY],
        out_specs=[VMEM] * 3,
        out_shape=[out] * 3,
        scratch_shapes=[pltpu.SemaphoreType.DMA((3,))],
    )(here, entries)


def pick_start(use, sources, target, sem):
    for q, source in enumerate(sources):

        @pl.when(use == q)
        def _(source=source):
            pltpu.make_async_copy(source, target, sem).start()

    return pltpu.make_async_copy(sources[-1], target, sem)


def corner_split_kernel(here, entries, p0, p1, p2, o0, o1, o2, o3, buffer, sem):
    pick_start(here[2], (entries.at[:, 0], p0, p1, p2), buffer, sem).wait()
    for r, out in enumerate((o0, o1, o2, o3)):
        out[...] = buffer[:, r * CORNER_OFF : (r + 1) * CORNER_OFF, :]


def corner_split_call(here, entries, parts):
    out = jax.ShapeDtypeStruct((8, CORNER_OFF, B), F32)
    return pl.pallas_call(
        corner_split_kernel,
        name="corner_split",
        in_specs=[SMEM] + [ANY] * 4,
        out_specs=[VMEM] * 4,
        out_shape=[out] * 4,
        scratch_shapes=[pltpu.VMEM(parts[0].shape, F32), pltpu.SemaphoreType.DMA],
    )(here, entries, *parts)


def share_kernel(here, kids, entries, *refs):
    parts, corner_e, landed = refs[:3], refs[3:7], refs[7:15]
    row_out, col_out, corner_out, corner, sem = refs[15:]
    row = here[1]
    col = here[2]
    sources = (entries.at[:, 0], *parts)
    from_row = jnp.where(col == 0, 0, 1 + lax.rem(col + 3 - row, 3))
    from_col = jnp.where(row == 0, 0, 1 + lax.rem(col + 5 - row, 3))
    picks = (
        pick_start(from_row, sources, row_out, sem.at[0]),
        pick_start(from_col, sources, col_out, sem.at[1]),
        pick_start(row, corner_e, corner, sem.at[2]),
    )
    for pick in picks:
        pick.wait()
    for n, (t, u) in enumerate(LOWER):
        corner_out[n] = corner[t, :, u * TILE : (u + 1) * TILE]

    for d in range(8):
        add_share(row, col, kids, landed[d], 2 * d, row_out, col_out, corner_out)


def add_share(row, col, kids, landed, begin, row_out, col_out, corner_out):
    def add(at_piece, carry):
        n = begin + at_piece
        for h in range(2):
            for v in range(2):
                lanes = slice(v * TILE, (v + 1) * TILE)
                t = kids[n, 2 * row + h] - 8 * row
                u = pl.ds(pl.multiple_of(kids[n, v] * TILE, TILE), TILE)
                row_out[t, :, u] += landed[at_piece, h * PANEL_OFF : (h + 1) * PANEL_OFF, lanes]
                t = kids[n, h]
                u = pl.ds(pl.multiple_of((kids[n, 2 * col + v] - 8 * col) * TILE, TILE), TILE)
                col_out[t, :, u] += landed[at_piece, (2 + h) * PANEL_OFF : (3 + h) * PANEL_OFF, lanes]
                if v <= h:
                    at = 4 * PANEL_OFF + h * CORNER_OFF
                    index = lax.shift_right_logical(t * (t + 1), 1) + kids[n, v]
                    corner_out[index] += landed[at_piece, at : at + CORNER_OFF, lanes]
        return carry

    lax.fori_loop(0, 2, add, 0)


def share_call(here, kids, entries, parts, corner_e, landed):
    panel = parts[0].shape
    corner = (len(LOWER), CORNER_OFF, TILE)
    return pl.pallas_call(
        share_kernel,
        name="share_assembly",
        in_specs=[SMEM, SMEM] + [ANY] * 8 + [VMEM] * 8,
        out_specs=[VMEM] * 3,
        out_shape=[
            jax.ShapeDtypeStruct(panel, F32),
            jax.ShapeDtypeStruct(panel, F32),
            jax.ShapeDtypeStruct(corner, F32),
        ],
        scratch_shapes=[pltpu.VMEM(corner_e[0].shape, F32), pltpu.SemaphoreType.DMA((3,))],
    )(here, kids, entries, *parts, *corner_e, *landed)


def corner_kernel(parts, l, invs, a, hi, lo, col, tile, u, inv):
    for d in range(16):
        off = (4 * (d % 4) + d // 4) * CORNER_OFF
        for n, (t, v) in enumerate(LOWER):
            at = t * TILE + off
            a[at : at + CORNER_OFF, v * TILE : (v + 1) * TILE] = parts[d, n]

    def done(b):
        invs[b] = inv[...]

    factor_columns(a, l, hi, lo, col, tile, u, inv, lambda b: None, done)


def corner_call(parts):
    return pl.pallas_call(
        corner_kernel,
        name="corner_factor",
        in_specs=[VMEM],
        out_specs=[VMEM, VMEM],
        out_shape=[
            jax.ShapeDtypeStruct((E, E), F32),
            jax.ShapeDtypeStruct((E // TILE, TILE, TILE), F32),
        ],
        scratch_shapes=[
            pltpu.VMEM((E, E), F32),
            pltpu.VMEM((E, E), BF16),
            pltpu.VMEM((E, E), BF16),
            pltpu.VMEM((E, TILE), F32),
            pltpu.VMEM((TILE, TILE), F32),
            pltpu.VMEM((TILE, TILE), F32),
            pltpu.VMEM((TILE, TILE), F32),
        ],
    )(parts)


def copy_rows(source, target):
    def chunk(c, carry):
        part = pl.ds(pl.multiple_of(c * TILE, TILE), TILE)
        target[part, :] = source[part, :]
        return carry

    lax.fori_loop(0, source.shape[0] // TILE, chunk, 0)


def parent_kernel(here, kids, l, invs, *refs):
    row_parts, col_parts = refs[:4], refs[4:8]
    entries, landed, out, a, b, whi, wlo, yhi, ylo, block, pieces, sem = refs[8:]
    row = here[1]
    col = here[2]
    loads = (
        pltpu.make_async_copy(entries, block, sem.at[0]),
        pltpu.make_async_copy(landed, pieces, sem.at[1]),
    )
    for load in loads:
        load.start()

    def arrange(t, carry):
        for s in range(4):
            for target, parts, place in ((a, row_parts, col), (b, col_parts, row)):
                at = t * TILE + ((place + 4 - s) & 3) * PANEL_OFF
                target[pl.ds(pl.multiple_of(at, PANEL_OFF), PANEL_OFF), :] = parts[s][t]
        return carry

    lax.fori_loop(0, 8, arrange, 0)
    wide = 2 * TILE
    for k in range(E // wide):
        at = k * wide
        mid = at + TILE
        here_k = slice(at, at + wide)
        first = split(invs[2 * k])
        second = split(invs[2 * k + 1])
        below = split(dot3(second, split(l[mid : at + wide, at:mid]), NN))
        below = -dot3(below, first, NN)
        zero = jnp.zeros((TILE, TILE), F32)
        inv = split(
            jnp.concatenate(
                [
                    jnp.concatenate([invs[2 * k], zero], 1),
                    jnp.concatenate([below, invs[2 * k + 1]], 1),
                ],
                0,
            )
        )
        lower = split(l[here_k, :at]) if k else None

        def chunk(c, carry):
            part = pl.ds(pl.multiple_of(c * CHUNK, CHUNK), CHUNK)
            left = a[part, here_k]
            right = b[here_k, part]
            if k:
                left = left - dot3((whi[part, :at], wlo[part, :at]), lower, NT)
                right = right - dot3(lower, (yhi[:at, part], ylo[:at, part]), NN)
            left = dot3(split(left), inv, NT)
            right = dot3(inv, split(right), NN)
            a[part, here_k] = left
            b[here_k, part] = right
            whi[part, here_k], wlo[part, here_k] = split(left)
            yhi[here_k, part], ylo[here_k, part] = split(right)
            return carry

        lax.fori_loop(0, B // CHUNK, chunk, 0)
    for load in loads:
        load.wait()

    @pl.when((row == 0) & (col == 0))
    def _():
        copy_rows(l, out)

    @pl.when((row != 0) & (col == 0))
    def _():
        copy_rows(a, out)

    @pl.when((row == 0) & (col != 0))
    def _():
        copy_rows(b, out)

    @pl.when((row != 0) & (col != 0))
    def _():
        def chunk(c, carry):
            part = pl.ds(pl.multiple_of(c * CHUNK, CHUNK), CHUNK)
            right = (yhi[...], ylo[...])
            out[part, :] = block[part, :] - dot3((whi[part, :], wlo[part, :]), right, NN)
            return carry

        lax.fori_loop(0, B // CHUNK, chunk, 0)

        def add(n, carry):
            plane = lax.shift_right_logical(n, 1)
            child = 2 * ((here[0] + 8 - plane) & 7) + (n & 1)
            for h in range(2):
                for v in range(2):
                    t = pl.multiple_of((kids[child, 2 * row + h] - 8 * row) * TILE, TILE)
                    u = pl.multiple_of((kids[child, 2 * col + v] - 8 * col) * TILE, TILE)
                    out[pl.ds(t, TILE), pl.ds(u, TILE)] += pieces[
                        n, h * TILE : (h + 1) * TILE, v * TILE : (v + 1) * TILE
                    ]
            return carry

        lax.fori_loop(0, 16, add, 0)


def parent_call(here, kids, l, invs, row_parts, col_parts, entries, landed):
    return pl.pallas_call(
        parent_kernel,
        name="parent",
        in_specs=[SMEM, SMEM] + [VMEM] * 10 + [ANY] * 2,
        out_specs=VMEM,
        out_shape=jax.ShapeDtypeStruct((B, B), F32),
        scratch_shapes=[pltpu.VMEM((B, E), F32)] * 2
        + [pltpu.VMEM((B, E), BF16)] * 4
        + [
            pltpu.VMEM((B, B), F32),
            pltpu.VMEM(landed.shape, F32),
            pltpu.SemaphoreType.DMA((2,)),
        ],
    )(here, kids, l, invs, *row_parts, *col_parts, entries, landed)


def exchange(array, axes):
    return lax.all_to_all(array, axes, split_axis=0, concat_axis=0, tiled=True)


def shifts(array, axis):
    parts = [array]
    for s in range(1, 4):
        if axis == "col":
            perm = [(4 * i + j, 4 * i + (j + s) % 4) for i in range(1, 4) for j in range(4)]
        else:
            perm = [(4 * i + j, 4 * ((i + s) % 4) + j) for i in range(4) for j in range(1, 4)]
        parts.append(lax.ppermute(array, ("row", "col"), perm))
    return parts


def hand_out(packed):
    out = []
    for s in range(3):
        perm = [(0, 1 + s)]
        for i in range(3):
            perm.append((4 * (1 + i), 4 * (1 + i) + 1 + (i + s) % 3))
            perm.append((1 + i, 4 * (1 + (i - s - 1) % 3) + 1 + i))
        out.append(lax.ppermute(packed[s], ("row", "col"), perm))
    return out


def from_first(parts, axis):
    out = [parts[0]]
    for q in range(1, 4):
        out.append(lax.ppermute(parts[q], axis, [(0, q)]))
    return out


def program(child_fronts, parent_entries, tile_map, parent_group):
    plane = ("row", "col")
    front = child_fronts[0]
    entries = parent_entries[0]
    here = jnp.stack([lax.axis_index(name) for name in ("front", "row", "col")]).astype(jnp.int32)
    label = jnp.concatenate([tile_map[0], parent_group, jnp.zeros((PIECE - 9,), jnp.int32)])
    label = jnp.broadcast_to(label.astype(F32)[None], (8, PIECE))
    by_offset = entries.reshape(8, 4, PANEL_OFF, B)
    packed = pack_call(here, by_offset)
    parts_e = hand_out(packed)
    factor, share = child_call(front, label)
    pieces = update_call(front, factor)
    share_near = exchange(share, plane)
    corner_e = corner_split_call(here, by_offset, parts_e)
    corner_e = from_first(corner_e, "row")
    labels = share_near[:, LABEL_ROW, :16].astype(jnp.int32)
    dealt = deal_call(here, labels, share_near)
    landed = [dealt[0]]
    for d in range(1, 8):
        landed.append(lax.ppermute(dealt[d], "front", [(f, (f + d) % 8) for f in range(8)]))
    kids = jnp.concatenate([part[:, LABEL_ROW, :8] for part in landed]).astype(jnp.int32)
    pieces_near = exchange(pieces, plane)
    pieces_near = regroup_call(labels, pieces_near)
    pieces_far = exchange(pieces_near, "front")
    row_own, col_own, corner_own = share_call(here, kids, by_offset, parts_e, corner_e, landed)
    corner_parts = lax.all_gather(corner_own, plane)
    row_parts = shifts(row_own, "col")
    col_parts = shifts(col_own, "row")
    l, invs = corner_call(corner_parts)
    result = parent_call(here, kids, l, invs, row_parts, col_parts, entries, pieces_far)
    return (factor[None], result[None])


def solution(mesh):
    in_specs = (
        P(("front", "row", "col"), None, None),
        P("front", "row", "col"),
        P(("front", "row", "col"), None),
        P(("front", "row", "col")),
    )
    out_specs = (P(("front", "row", "col"), None, None), P("front", "row", "col"))
    return jax.shard_map(program, mesh=mesh, in_specs=in_specs, out_specs=out_specs, check_vma=False)
```
